32 devices in a mesh: nodes: 16 (over z, y, x), feat: 2 (over core).
Axes of the slice: x: 2, y: 2, z: 4, core: 2. Of those that a mesh axis runs over, the one named last changes fastest.
Arguments:
- grid_latent: bfloat16 [16384, 512], P('nodes', 'feat'), may hold values from -6 to 6
- mesh_latent: bfloat16 [16384, 512], P('nodes', 'feat'), may hold values from -6 to 6
- grid_order: int32 [16, 1024], P('nodes'), may hold values from 0 to 1023, each once within a row
- enc_send_block: int32 [256], P('nodes'), may hold values from 0 to 7
- enc_recv_block: int32 [256], P('nodes'), may hold values from 0 to 7
- enc_offsets: int32 [256, 2, 128], P('nodes'), may hold values from 0 to 127
- enc_classes: int32 [256, 128], P('nodes'), may hold values from 0 to 7
- enc_live: int32 [16], P('nodes'), may hold values from 1 to 16, 160 in all
- mesh_send_block: int32 [1536], P('nodes'), may hold values from 0 to 23
- mesh_recv_block: int32 [1536], P('nodes'), may hold values from 0 to 7
- mesh_offsets: int32 [1536, 2, 128], P('nodes'), may hold values from 0 to 127
- mesh_classes: int32 [1536, 128], P('nodes'), may hold values from 0 to 7
- mesh_live: int32 [16], P('nodes'), may hold values from 1 to 96, 960 in all
- dec_send_block: int32 [384], P('nodes'), may hold values from 0 to 7
- dec_recv_block: int32 [384], P('nodes'), may hold values from 0 to 7
- dec_offsets: int32 [384, 2, 128], P('nodes'), may hold values from 0 to 127
- dec_classes: int32 [384, 128], P('nodes'), may hold values from 0 to 7
- dec_live: int32 [16], P('nodes'), may hold values from 1 to 24, 240 in all
- class_gain: float32 [3, 8], replicated, may hold values from 0.25 to 2
- enc_weights: bfloat16 [3, 512, 512], P(None, None, 'feat'), may hold values from -0.25 to 0.25
- mesh_weights: bfloat16 [2, 3, 512, 512], P(None, None, None, 'feat'), may hold values from -0.25 to 0.25
- dec_weights: bfloat16 [3, 512, 512], P(None, None, 'feat'), may hold values from -0.25 to 0.25
- enc_bias: float32 [512], P('feat'), may hold values from -3 to 3
- enc_gain: float32 [512], P('feat'), may hold values from 0.25 to 1.75
- mesh_bias: float32 [2, 512], P(None, 'feat'), may hold values from -3 to 3
- mesh_gain: float32 [2, 512], P(None, 'feat'), may hold values from 0.25 to 1.75
- dec_bias: float32 [512], P('feat'), may hold values from -3 to 3
- dec_gain: float32 [512], P('feat'), may hold values from 0.25 to 1.75
Outputs:
- grid_out: bfloat16 [16384, 512], P('nodes', 'feat')
- mesh_final: bfloat16 [16384, 512], P('nodes', 'feat')
The draws below stay inside these ranges and needn't reach their ends.
Inputs may be any that keep to these rules, and one draw needn't show every extreme that they name: Each row of grid_order lists each of 0..1023 once. The first enc_live[d] edge blocks of region d are live; the most is reached on some region. The first mesh_live[d] edge blocks of region d are live; the most is reached on some region. The first dec_live[d] edge blocks of region d are live; the most is reached on some region.
All inputs are finite; a program needn't handle non-finite values.
Results may differ from the reference program's by a relative error of at most 0.0085.
Values may be sent and summed in bfloat16 or wider, within the bound.
No kernel may reach another device: no remote copies, remote signals or barrier semaphores. Data moves between devices by JAX's collectives and lax.ppermute only.
A program may use at most 64 MiB of HBM per device.

```python
import math
import jax
import jax.numpy as jnp
import numpy as np
from jax import lax

D = 512
GRID_DEV = 1024
MESH_DEV = 1024
BLOCK = 128
ROUNDS = 2
NCLASS = 8
GRID = 16384
MESH = 16384
EB_ENC = 16
EB_MESH = 96
EB_DEC = 24
N_NODES = 16


def plant(array, rng, least, high):
    longest = array.shape.index(max(array.shape))
    spots = []
    for shift in (0, 1):
        where = [jax.random.randint(jax.random.fold_in(rng, axis), (), 0, length) for axis, length in enumerate(array.shape)]
        where[longest] = (where[longest] + shift) % array.shape[longest]
        spots.append(tuple(where))
    return array.at[spots[0]].set(least).at[spots[1]].set(high)


def steps_of(stream_key, shape, cuts, least, top_value):
    def one(position, blocks):
        heights = jax.random.uniform(jax.random.fold_in(jax.random.fold_in(stream_key, 6), position), (blocks,), jnp.float32, least / len(cuts), top_value / len(cuts))
        return jnp.repeat(jnp.exp(heights), shape[position] // blocks).reshape((-1,) + (1,) * (len(shape) - position - 1))

    gain = one(*cuts[0])
    for cut in cuts[1:]:
        gain = gain * one(*cut)
    return gain


def length_profile(amount, total, most, skew):
    loads = [(1 << 20) // math.isqrt(rank ** skew) + 1 for rank in range(2, amount + 1)]
    surplus, given = total - most - (amount - 1), [1] * (amount - 1)
    while surplus > 0:
        candidates = [i for i in range(amount - 1) if given[i] < most]
        whole, left = sum([loads[i] for i in candidates]), surplus
        for i in candidates:
            addition = min(most - given[i], max(1, left * loads[i] // whole), surplus)
            given[i] = given[i] + addition
            surplus = surplus - addition
    return np.array([most] + given)


def ragged_sizes(key, amount, total, limit, slope):
    if amount == 2:
        one = jax.random.randint(key, (), max(1, total - limit), min(limit, total - 1) + 1)
        return jnp.stack([one, total - one])
    lengths = jnp.asarray(length_profile(amount, total, limit, slope), jnp.int32)
    couples = (amount - 1) // 2
    source_of, sink = lengths[1:1 + 2 * couples:2], lengths[2:2 + 2 * couples:2]
    room = jnp.minimum(source_of - 1, limit - sink)
    shifted = jax.random.randint(jax.random.fold_in(key, 1), (couples,), 0, 1 << 20) % (room + 1)
    lengths = lengths.at[1:1 + 2 * couples:2].set(source_of - shifted).at[2:2 + 2 * couples:2].set(sink + shifted)
    return lengths[jax.random.permutation(jax.random.fold_in(key, 2), amount)]


def bell_draw(own_key, extent, width, most, cuts=(), held_as=jnp.bfloat16):
    entries = width * jax.random.normal(own_key, extent, jnp.float32)
    if cuts:
        entries = entries * steps_of(own_key, extent, cuts, -0.22, 0.18)
    return jnp.clip(entries, -most, most).astype(held_as)


def setup_inputs(seed: int = 0) -> dict:
    keys = jax.random.split(jax.random.key(seed), 29)
    grid_latent = bell_draw(keys[0], (GRID, D), 1.0, 6.0, ((0, 16), (1, 2)))
    mesh_latent = bell_draw(keys[1], (MESH, D), 1.0, 6.0, ((0, 16), (1, 2)))
    grid_order = jax.vmap(lambda own: jax.random.permutation(own, GRID_DEV))(jax.random.split(keys[2], N_NODES)).reshape((N_NODES, GRID_DEV)).astype(jnp.int32)
    enc_send_block = plant(jax.random.randint(keys[3], (N_NODES * EB_ENC,), 0, GRID_DEV // BLOCK), jax.random.fold_in(keys[3], 1), 0, (GRID_DEV // BLOCK) - 1).astype(jnp.int32)
    enc_recv_block = plant(jax.random.randint(keys[4], (N_NODES * EB_ENC,), 0, MESH_DEV // BLOCK), jax.random.fold_in(keys[4], 1), 0, (MESH_DEV // BLOCK) - 1).astype(jnp.int32)
    enc_offsets = plant(jax.random.randint(keys[5], (N_NODES * EB_ENC, 2, BLOCK), 0, BLOCK), jax.random.fold_in(keys[5], 1), 0, BLOCK - 1).astype(jnp.int32)
    enc_classes = plant(jax.random.randint(keys[6], (N_NODES * EB_ENC, BLOCK), 0, NCLASS), jax.random.fold_in(keys[6], 1), 0, NCLASS - 1).astype(jnp.int32)
    enc_live = ragged_sizes(keys[7], N_NODES, N_NODES * EB_ENC * 5 // 8, EB_ENC, 2).astype(jnp.int32)
    mesh_send_block = plant(jax.random.randint(keys[8], (N_NODES * EB_MESH,), 0, 3 * MESH_DEV // BLOCK), jax.random.fold_in(keys[8], 1), 0, (3 * MESH_DEV // BLOCK) - 1).astype(jnp.int32)
    mesh_recv_block = plant(jax.random.randint(keys[9], (N_NODES * EB_MESH,), 0, MESH_DEV // BLOCK), jax.random.fold_in(keys[9], 1), 0, (MESH_DEV // BLOCK) - 1).astype(jnp.int32)
    mesh_offsets = plant(jax.random.randint(keys[10], (N_NODES * EB_MESH, 2, BLOCK), 0, BLOCK), jax.random.fold_in(keys[10], 1), 0, BLOCK - 1).astype(jnp.int32)
    mesh_classes = plant(jax.random.randint(keys[11], (N_NODES * EB_MESH, BLOCK), 0, NCLASS), jax.random.fold_in(keys[11], 1), 0, NCLASS - 1).astype(jnp.int32)
    mesh_live = ragged_sizes(keys[12], N_NODES, N_NODES * EB_MESH * 5 // 8, EB_MESH, 2).astype(jnp.int32)
    dec_send_block = plant(jax.random.randint(keys[13], (N_NODES * EB_DEC,), 0, MESH_DEV // BLOCK), jax.random.fold_in(keys[13], 1), 0, (MESH_DEV // BLOCK) - 1).astype(jnp.int32)
    dec_recv_block = plant(jax.random.randint(keys[14], (N_NODES * EB_DEC,), 0, GRID_DEV // BLOCK), jax.random.fold_in(keys[14], 1), 0, (GRID_DEV // BLOCK) - 1).astype(jnp.int32)
    dec_offsets = plant(jax.random.randint(keys[15], (N_NODES * EB_DEC, 2, BLOCK), 0, BLOCK), jax.random.fold_in(keys[15], 1), 0, BLOCK - 1).astype(jnp.int32)
    dec_classes = plant(jax.random.randint(keys[16], (N_NODES * EB_DEC, BLOCK), 0, NCLASS), jax.random.fold_in(keys[16], 1), 0, NCLASS - 1).astype(jnp.int32)
    dec_live = ragged_sizes(keys[17], N_NODES, N_NODES * EB_DEC * 5 // 8, EB_DEC, 2).astype(jnp.int32)
    class_gain = jnp.clip(jnp.exp(jax.random.uniform(keys[18], (3, NCLASS), jnp.float32, math.log(0.25), math.log(2.0))), 0.25, 2.0)
    enc_weights = bell_draw(keys[19], (3, D, D), D ** -0.5, 0.25, ((2, 2),))
    mesh_weights = bell_draw(keys[20], (ROUNDS, 3, D, D), D ** -0.5, 0.25, ((3, 2),))
    dec_weights = bell_draw(keys[21], (3, D, D), D ** -0.5, 0.25, ((2, 2),))
    enc_bias = bell_draw(keys[22], (D,), 0.5, 3.0, ((0, 2),), jnp.float32)
    enc_gain = jnp.clip(1.0 + 0.15 * jax.random.normal(keys[23], (D,), jnp.float32), 0.25, 1.75)
    mesh_bias = bell_draw(keys[24], (ROUNDS, D), 0.5, 3.0, ((1, 2),), jnp.float32)
    mesh_gain = jnp.clip(1.0 + 0.15 * jax.random.normal(keys[25], (ROUNDS, D), jnp.float32), 0.25, 1.75)
    dec_bias = bell_draw(keys[26], (D,), 0.5, 3.0, ((0, 2),), jnp.float32)
    dec_gain = jnp.clip(1.0 + 0.15 * jax.random.normal(keys[27], (D,), jnp.float32), 0.25, 1.75)
    return {"grid_latent": grid_latent, "mesh_latent": mesh_latent, "grid_order": grid_order, "enc_send_block": enc_send_block, "enc_recv_block": enc_recv_block, "enc_offsets": enc_offsets, "enc_classes": enc_classes, "enc_live": enc_live, "mesh_send_block": mesh_send_block, "mesh_recv_block": mesh_recv_block, "mesh_offsets": mesh_offsets, "mesh_classes": mesh_classes, "mesh_live": mesh_live, "dec_send_block": dec_send_block, "dec_recv_block": dec_recv_block, "dec_offsets": dec_offsets, "dec_classes": dec_classes, "dec_live": dec_live, "class_gain": class_gain, "enc_weights": enc_weights, "mesh_weights": mesh_weights, "dec_weights": dec_weights, "enc_bias": enc_bias, "enc_gain": enc_gain, "mesh_bias": mesh_bias, "mesh_gain": mesh_gain, "dec_bias": dec_bias, "dec_gain": dec_gain}


epsilon = 1e-05

def project(inputs, matrix):
    return jnp.dot(inputs, matrix, preferred_element_type=jnp.float32)

def normed(mixed, gain_vector):
    average = lax.optimization_barrier(jnp.mean(mixed, axis=-1, keepdims=True))
    spread = lax.optimization_barrier(jnp.mean(mixed * mixed, axis=-1, keepdims=True)) - average * average
    return (mixed - average) * lax.rsqrt(spread + epsilon) * gain_vector

def edge_sum(sender, receiver, bias_row, class_row, send_ids, recv_ids, offset_pair, labels, live_count, row_count):
    slots = send_ids.shape[0]
    sender_rows = send_ids[:, None] * BLOCK + offset_pair[:, 0, :]
    taker_rows = recv_ids[:, None] * BLOCK + offset_pair[:, 1, :]
    living = (jnp.arange(slots, dtype=jnp.int32) < live_count).astype(jnp.float32)
    weight = class_row[labels] * living[:, None]
    summed = sender[sender_rows].astype(jnp.float32) + receiver[taker_rows].astype(jnp.float32) + bias_row
    message = (jax.nn.silu(summed) * weight[:, :, None]).astype(jnp.bfloat16)
    flat = message.reshape(-1, message.shape[-1]).astype(jnp.float32)
    return jax.ops.segment_sum(flat, taker_rows.reshape(-1), num_segments=row_count)

def refresh(residual, gathered, matrix, gain_vector):
    mixed = project(gathered.reshape(-1, D).astype(jnp.bfloat16), matrix)
    return (residual.astype(jnp.float32) + normed(mixed, gain_vector)).astype(jnp.bfloat16)

def reference(grid_latent, mesh_latent, grid_order, enc_send_block, enc_recv_block, enc_offsets, enc_classes, enc_live, mesh_send_block, mesh_recv_block, mesh_offsets, mesh_classes, mesh_live, dec_send_block, dec_recv_block, dec_offsets, dec_classes, dec_live, class_gain, enc_weights, mesh_weights, dec_weights, enc_bias, enc_gain, mesh_bias, mesh_gain, dec_bias, dec_gain):
    node_count = N_NODES
    per_peer = GRID_DEV // node_count
    routing = grid_order.reshape(node_count, node_count, per_peer) + (jnp.arange(node_count, dtype=jnp.int32) * GRID_DEV)[:, None, None]
    received = jnp.transpose(routing, (1, 0, 2)).reshape(node_count, GRID_DEV)
    send_proj = project(grid_latent, enc_weights[0]).astype(jnp.bfloat16)
    grid_proj = project(grid_latent, dec_weights[1]).astype(jnp.bfloat16)
    mesh_proj = project(mesh_latent, enc_weights[1]).astype(jnp.bfloat16).reshape(node_count, MESH_DEV, D)

    def encode(pieces):
        rows_index, receiver, send_ids, recv_ids, offset_pair, labels, live_count = pieces
        return edge_sum(send_proj[rows_index], receiver, enc_bias, class_gain[0], send_ids, recv_ids, offset_pair, labels, live_count, MESH_DEV)
    enc_agg = lax.map(encode, (received, mesh_proj, enc_send_block.reshape(node_count, -1), enc_recv_block.reshape(node_count, -1), enc_offsets.reshape(node_count, -1, 2, BLOCK), enc_classes.reshape(node_count, -1, BLOCK), enc_live))
    mesh = refresh(mesh_latent, enc_agg, enc_weights[2], enc_gain)
    for round_index in range(ROUNDS):
        weights = mesh_weights[round_index]
        round_bias = mesh_bias[round_index]
        sending = project(mesh, weights[0]).astype(jnp.bfloat16).reshape(node_count, MESH_DEV, D)
        taking = project(mesh, weights[1]).astype(jnp.bfloat16).reshape(node_count, MESH_DEV, D)
        nearby = jnp.concatenate([jnp.roll(sending, 1, axis=0), sending, jnp.roll(sending, -1, axis=0)], axis=1)

        def relay(pieces):
            sender, receiver, send_ids, recv_ids, offset_pair, labels, live_count = pieces
            return edge_sum(sender, receiver, round_bias, class_gain[1], send_ids, recv_ids, offset_pair, labels, live_count, MESH_DEV)
        mesh_agg = lax.map(relay, (nearby, taking, mesh_send_block.reshape(node_count, -1), mesh_recv_block.reshape(node_count, -1), mesh_offsets.reshape(node_count, -1, 2, BLOCK), mesh_classes.reshape(node_count, -1, BLOCK), mesh_live))
        mesh = refresh(mesh, mesh_agg, weights[2], mesh_gain[round_index])
    dec_proj = project(mesh, dec_weights[0]).astype(jnp.bfloat16).reshape(node_count, MESH_DEV, D)

    def decode(pieces):
        rows_index, sender, send_ids, recv_ids, offset_pair, labels, live_count = pieces
        return edge_sum(sender, grid_proj[rows_index], dec_bias, class_gain[2], send_ids, recv_ids, offset_pair, labels, live_count, GRID_DEV)
    dec_agg = lax.map(decode, (received, dec_proj, dec_send_block.reshape(node_count, -1), dec_recv_block.reshape(node_count, -1), dec_offsets.reshape(node_count, -1, 2, BLOCK), dec_classes.reshape(node_count, -1, BLOCK), dec_live))
    mixed = project(dec_agg.reshape(-1, D).astype(jnp.bfloat16), dec_weights[2])
    update = normed(mixed, dec_gain).astype(jnp.bfloat16)
    placed = jnp.zeros_like(grid_latent).at[received.reshape(-1)].set(update)
    grid_out = (grid_latent.astype(jnp.float32) + placed.astype(jnp.float32)).astype(jnp.bfloat16)
    return (grid_out, mesh)
```

```python
import functools

import jax
import jax.numpy as jnp
from jax import lax
from jax.experimental import pallas as pl
from jax.experimental.pallas import tpu as pltpu
from jax.sharding import PartitionSpec as P

BLOCK = 128
ROUNDS = 2
UNROLL = 4
EPSILON = 1e-05

VMEM = pl.BlockSpec(memory_space=pltpu.VMEM)
SMEM = pl.BlockSpec(memory_space=pltpu.SMEM)
F32 = jnp.float32
BF16 = jnp.bfloat16


def dot(a, b):
    return jnp.dot(a, b, preferred_element_type=F32)


def params(mib=24):
    return pltpu.CompilerParams(vmem_limit_bytes=mib << 20)


def pieces(rows):
    return min(rows, 256)


def entry(slot, sender, taker, total):
    return slot + sender * 256 + taker * 65536 + total * 16777216


def list_length(slots):
    return slots + UNROLL


def list_kernel(
    blocks,
    parity,
    gains,
    es,
    er,
    el,
    ec,
    ms,
    mr,
    ml,
    mc,
    ds,
    dr,
    dl,
    dc,
    e_list,
    m_list,
    d_list,
    counts,
    e_w,
    m_w,
    d_w,
):
    def finish(out, base, count):
        for k in range(UNROLL):
            out[base + count + k] = entry(0, 0, 0, blocks)
        return (count + UNROLL - 1) // UNROLL

    def plain(sends, takes, live, out, where):
        total = live[0]

        def step(i, carry):
            taker = takes[i]
            out[i] = entry(i, sends[i], taker, taker)
            return carry

        lax.fori_loop(0, total, step, 0)
        counts[where] = finish(out, 0, total)

    plain(es, er, el, e_list, 0)
    plain(ds, dr, dl, d_list, 1)
    length = list_length(ms.shape[0])
    first = jnp.where(parity[0] == 0, 2, 0)

    def step(i, carry):
        own, near, far = carry
        sender = ms[i]
        taker = mr[i]
        group = sender // blocks
        is_own = group == 1
        is_near = group == first
        place = jnp.where(
            is_own, own, jnp.where(is_near, length + near, 2 * length + far)
        )
        m_list[place] = entry(i, sender - group * blocks, taker, taker)
        own_up = is_own.astype(jnp.int32)
        near_up = is_near.astype(jnp.int32)
        return own + own_up, near + near_up, far + 1 - own_up - near_up

    zero = jnp.int32(0)
    own, near, far = lax.fori_loop(0, ml[0], step, (zero, zero, zero))
    counts[2] = finish(m_list, 0, own)
    counts[3] = finish(m_list, length, near)
    counts[4] = finish(m_list, 2 * length, far)
    for index, (labels, out) in enumerate(((ec, e_w), (mc, m_w), (dc, d_w))):
        marks = labels[...]
        weight = jnp.zeros(marks.shape, F32)
        for k in range(gains.shape[1]):
            weight = jnp.where(marks == k, gains[index, k], weight)
        out[...] = weight


def edge_lists(blocks, parity, gains, enc, mesh, dec):
    i32 = jnp.int32
    lengths = [list_length(enc[0].shape[0]), 3 * list_length(mesh[0].shape[0])]
    lengths.append(list_length(dec[0].shape[0]))
    out_shape = [jax.ShapeDtypeStruct((n,), i32) for n in lengths]
    out_shape.append(jax.ShapeDtypeStruct((8,), i32))
    out_shape += [jax.ShapeDtypeStruct(s[3].shape, F32) for s in (enc, mesh, dec)]
    return pl.pallas_call(
        functools.partial(list_kernel, blocks),
        out_shape=out_shape,
        in_specs=[SMEM, SMEM] + [SMEM, SMEM, SMEM, VMEM] * 3,
        out_specs=[SMEM] * 4 + [VMEM] * 3,
        compiler_params=params(8),
    )(parity, gains, *enc, *mesh, *dec)


def edge_loop(base, trips, items, send, take, offsets, weights, acc):
    rows = lax.broadcasted_iota(jnp.int32, (BLOCK, BLOCK), 0)
    one = jnp.ones((BLOCK, BLOCK), F32)
    nil = jnp.zeros((BLOCK, BLOCK), F32)

    def one_block(position):
        item = items[position]
        slot = item & 255
        sender = pl.multiple_of(((item >> 8) & 255) * BLOCK, BLOCK)
        taker = pl.multiple_of(((item >> 16) & 255) * BLOCK, BLOCK)
        total = pl.multiple_of((item >> 24) * BLOCK, BLOCK)
        from_row = offsets[pl.ds(2 * slot, 1), :]
        to_row = offsets[pl.ds(2 * slot + 1, 1), :]
        weight = weights[pl.ds(slot, 1), :]
        is_from = rows == from_row
        is_to = rows == to_row
        pick = jnp.concatenate(
            [jnp.where(is_from, one, nil), jnp.where(is_to, one, nil)], axis=0
        ).astype(BF16)
        both = jnp.concatenate(
            [send[pl.ds(sender, BLOCK), :], take[pl.ds(taker, BLOCK), :]], axis=0
        )
        half = lax.dot_general(
            pick, both, (((0,), (0,)), ((), ())), preferred_element_type=F32
        )
        message = (half + half * jnp.tanh(half)).astype(BF16)
        spread = jnp.where(is_to, weight, nil).astype(BF16)
        acc[pl.ds(total, BLOCK), :] += dot(spread, message)

    def turn(i, carry):
        for u in range(UNROLL):
            one_block(base + i * UNROLL + u)
        return carry

    lax.fori_loop(0, trips, turn, 0)


def edge_kernel(where, base, first, last, counts, items, send, take, offsets, weights, *rest):
    rest = list(rest)
    before = None if first else rest.pop(0)
    out, acc = rest
    rows = out.shape[0]
    if first:
        acc[...] = jnp.zeros_like(acc)
    else:
        acc[pl.ds(0, rows), :] = before[...]
    edge_loop(base, counts[where], items, send, take, offsets, weights, acc)
    out[...] = acc[pl.ds(0, rows), :].astype(out.dtype)


def edge_sum(where, base, counts, items, send, take, offsets, weights, before, last):
    first = before is None
    rows, columns = take.shape
    arrays = [counts, items, send, take, offsets, weights]
    if not first:
        arrays.append(before)
    return pl.pallas_call(
        functools.partial(edge_kernel, where, base, first, last),
        out_shape=jax.ShapeDtypeStruct((rows, columns), BF16 if last else F32),
        in_specs=[SMEM, SMEM] + [VMEM] * (len(arrays) - 2),
        out_specs=VMEM,
        scratch_shapes=[pltpu.VMEM((rows + BLOCK, columns), F32)],
        compiler_params=params(),
        cost_estimate=pl.CostEstimate(
            flops=200_000_000, bytes_accessed=2_000_000, transcendentals=1_000_000
        ),
    )(*arrays)


def two_dots(a, b, weights, mine, other, width):
    return dot(a, weights[pl.ds(mine, width), :]) + dot(b, weights[pl.ds(other, width), :])


def normalized(ym, yt):
    width = ym.shape[1] + yt.shape[1]
    total = jnp.sum(ym, axis=1, keepdims=True) + jnp.sum(yt, axis=1, keepdims=True)
    squares = jnp.sum(ym * ym, axis=1, keepdims=True) + jnp.sum(
        yt * yt, axis=1, keepdims=True
    )
    mean = total / width
    spread = squares / width - mean * mean
    return mean, lax.rsqrt(spread + EPSILON)


def mix_kernel(
    core, am, at, xm, xt, wm, wt, gm, gt, ws, out_m, out_t, out_s
):
    rows, width = am.shape
    tile = pieces(rows)
    mine = pl.multiple_of(core[0] * width, width)
    other = pl.multiple_of(width - core[0] * width, width)

    def step(t, carry):
        part = pl.ds(pl.multiple_of(t * tile, tile), tile)
        a = am[part, :]
        b = at[part, :]
        ym = two_dots(a, b, wm, mine, other, width)
        yt = two_dots(a, b, wt, mine, other, width)
        mean, scale = normalized(ym, yt)
        nm = (xm[part, :].astype(F32) + (ym - mean) * scale * gm[...]).astype(BF16)
        nt = (xt[part, :].astype(F32) + (yt - mean) * scale * gt[...]).astype(BF16)
        out_m[part, :] = nm
        out_t[part, :] = nt
        out_s[part, :] = (0.5 * two_dots(nm, nt, ws, mine, other, width)).astype(BF16)
        return carry

    lax.fori_loop(0, rows // tile, step, 0)


def mix(core, am, at, xm, xt, wm, wt, gm, gt, ws):
    shape = jax.ShapeDtypeStruct(am.shape, BF16)
    return pl.pallas_call(
        mix_kernel,
        out_shape=[shape] * 3,
        in_specs=[SMEM] + [VMEM] * 9,
        out_specs=[VMEM] * 3,
        compiler_params=params(),
    )(core, am, at, xm, xt, wm, wt, gm, gt, ws)


def project_kernel(core, xm, xt, w, bias, out):
    rows, width = xm.shape
    tile = pieces(rows)
    mine = pl.multiple_of(core[0] * width, width)
    other = pl.multiple_of(width - core[0] * width, width)

    def step(t, carry):
        part = pl.ds(pl.multiple_of(t * tile, tile), tile)
        y = two_dots(xm[part, :], xt[part, :], w, mine, other, width)
        out[part, :] = (0.5 * (y + bias[...])).astype(BF16)
        return carry

    lax.fori_loop(0, rows // tile, step, 0)


def project(core, xm, xt, w, bias):
    return pl.pallas_call(
        project_kernel,
        out_shape=jax.ShapeDtypeStruct(xm.shape, BF16),
        in_specs=[SMEM] + [VMEM] * 4,
        out_specs=VMEM,
        compiler_params=params(),
    )(core, xm, xt, w, bias)


def update_kernel(core, am, at, wm, wt, gm, out):
    rows, width = am.shape
    tile = pieces(rows)
    mine = pl.multiple_of(core[0] * width, width)
    other = pl.multiple_of(width - core[0] * width, width)

    def step(t, carry):
        part = pl.ds(pl.multiple_of(t * tile, tile), tile)
        a = am[part, :]
        b = at[part, :]
        ym = two_dots(a, b, wm, mine, other, width)
        yt = two_dots(a, b, wt, mine, other, width)
        mean, scale = normalized(ym, yt)
        out[part, :] = ((ym - mean) * scale * gm[...]).astype(BF16)
        return carry

    lax.fori_loop(0, rows // tile, step, 0)


def update_of(core, am, at, wm, wt, gm):
    return pl.pallas_call(
        update_kernel,
        out_shape=jax.ShapeDtypeStruct(am.shape, BF16),
        in_specs=[SMEM] + [VMEM] * 5,
        out_specs=VMEM,
        compiler_params=params(),
    )(core, am, at, wm, wt, gm)


def pick_rows_kernel(order, x, out):
    rows = x.shape[0]
    tile = pieces(rows)

    def step(t, carry):
        part = pl.ds(pl.multiple_of(t * tile, tile), tile)
        ids = lax.broadcasted_iota(jnp.int32, (rows, tile), 0)
        chosen = jnp.where(ids == order[:, part], 1.0, 0.0).astype(BF16)
        out[part, :] = lax.dot_general(
            chosen, x[...], (((0,), (0,)), ((), ())), preferred_element_type=F32
        ).astype(BF16)
        return carry

    lax.fori_loop(0, rows // tile, step, 0)


def pick_rows(order, x):
    return pl.pallas_call(
        pick_rows_kernel,
        out_shape=jax.ShapeDtypeStruct(x.shape, BF16),
        in_specs=[VMEM] * 2,
        out_specs=VMEM,
        compiler_params=params(),
    )(order, x)


def place_rows_kernel(order, x, rest, out):
    rows = x.shape[0]
    tile = pieces(rows)

    def step(t, carry):
        start = pl.multiple_of(t * tile, tile)
        part = pl.ds(start, tile)
        ids = lax.broadcasted_iota(jnp.int32, (tile, rows), 0) + start
        chosen = jnp.where(ids == order[...], 1.0, 0.0).astype(BF16)
        out[part, :] = (rest[part, :].astype(F32) + dot(chosen, x[...])).astype(BF16)
        return carry

    lax.fori_loop(0, rows // tile, step, 0)


def place_rows(order, x, rest):
    return pl.pallas_call(
        place_rows_kernel,
        out_shape=jax.ShapeDtypeStruct(x.shape, BF16),
        in_specs=[VMEM] * 3,
        out_specs=VMEM,
        compiler_params=params(),
    )(order, x, rest)


def swap(x):
    return lax.ppermute(x, "feat", [(0, 1), (1, 0)])


def exchange(x):
    return lax.all_to_all(x, "nodes", split_axis=0, concat_axis=0, tiled=True)


def halo(send):
    size = lax.axis_size("nodes")
    near = lax.ppermute(send, "nodes", [(j, j ^ 1) for j in range(size)])
    onward = [(j, (j + 2 - 4 * (j % 2)) % size) for j in range(size)]
    far = lax.ppermute(near, "nodes", onward)
    return near, far


def local(
    grid_latent,
    mesh_latent,
    grid_order,
    enc_send_block,
    enc_recv_block,
    enc_offsets,
    enc_classes,
    enc_live,
    mesh_send_block,
    mesh_recv_block,
    mesh_offsets,
    mesh_classes,
    mesh_live,
    dec_send_block,
    dec_recv_block,
    dec_offsets,
    dec_classes,
    dec_live,
    class_gain,
    enc_weights,
    mesh_weights,
    dec_weights,
    enc_bias,
    enc_gain,
    mesh_bias,
    mesh_gain,
    dec_bias,
    dec_gain,
):
    rows = mesh_latent.shape[0]
    core = lax.axis_index("feat").astype(jnp.int32).reshape(1)
    parity = (lax.axis_index("nodes") % 2).astype(jnp.int32).reshape(1)
    arrived = exchange(pick_rows(grid_order, grid_latent))

    e_list, m_list, d_list, counts, e_w, m_w, d_w = edge_lists(
        rows // BLOCK,
        parity,
        class_gain,
        (enc_send_block, enc_recv_block, enc_live, enc_classes),
        (mesh_send_block, mesh_recv_block, mesh_live, mesh_classes),
        (dec_send_block, dec_recv_block, dec_live, dec_classes),
    )
    length = list_length(mesh_send_block.shape[0])
    e_off = enc_offsets.reshape(-1, BLOCK)
    m_off = mesh_offsets.reshape(-1, BLOCK)
    d_off = dec_offsets.reshape(-1, BLOCK)
    outs = [enc_weights[2], mesh_weights[0, 2], mesh_weights[1, 2], dec_weights[2]]
    outs_other = [swap(w) for w in outs]
    gains = jnp.stack([enc_gain, mesh_gain[0], mesh_gain[1]])
    gains_other = swap(gains)
    xm, xt = mesh_latent, swap(mesh_latent)
    take = project(core, xm, xt, enc_weights[1], enc_bias[None, :])

    arrived_other = swap(arrived)
    nothing = jnp.zeros((1, enc_bias.shape[0]), F32)
    send = project(core, arrived, arrived_other, enc_weights[0], nothing)
    agg = edge_sum(0, 0, counts, e_list, send, take, e_off, e_w, None, True)
    grid_take = project(core, arrived, arrived_other, dec_weights[1], dec_bias[None, :])
    for r in range(ROUNDS):
        xm, xt, send = mix(
            core,
            agg,
            swap(agg),
            xm,
            xt,
            outs[r],
            outs_other[r],
            gains[r : r + 1],
            gains_other[r : r + 1],
            mesh_weights[r, 0],
        )
        near, far = halo(send)
        take = project(core, xm, xt, mesh_weights[r, 1], mesh_bias[r][None, :])
        agg = edge_sum(2, 0, counts, m_list, send, take, m_off, m_w, None, False)
        agg = edge_sum(3, length, counts, m_list, near, take, m_off, m_w, agg, False)
        agg = edge_sum(4, 2 * length, counts, m_list, far, take, m_off, m_w, agg, True)
    xm, xt, send = mix(
        core,
        agg,
        swap(agg),
        xm,
        xt,
        outs[ROUNDS],
        outs_other[ROUNDS],
        gains[ROUNDS : ROUNDS + 1],
        gains_other[ROUNDS : ROUNDS + 1],
        dec_weights[0],
    )
    agg = edge_sum(1, 0, counts, d_list, send, grid_take, d_off, d_w, None, True)
    update = update_of(
        core, agg, swap(agg), outs[3], outs_other[3], dec_gain[None, :]
    )
    grid_out = place_rows(grid_order, exchange(update), grid_latent)
    return grid_out, xm


def solution(mesh):
    in_specs = (
        P("nodes", "feat"),
        P("nodes", "feat"),
        P("nodes", None),
        P("nodes"),
        P("nodes"),
        P("nodes", None, None),
        P("nodes", None),
        P("nodes"),
        P("nodes"),
        P("nodes"),
        P("nodes", None, None),
        P("nodes", None),
        P("nodes"),
        P("nodes"),
        P("nodes"),
        P("nodes", None, None),
        P("nodes", None),
        P("nodes"),
        P(),
        P(None, None, "feat"),
        P(None, None, None, "feat"),
        P(None, None, "feat"),
        P("feat"),
        P("feat"),
        P(None, "feat"),
        P(None, "feat"),
        P("feat"),
        P("feat"),
    )
    out_specs = (P("nodes", "feat"), P("nodes", "feat"))
    return jax.shard_map(local, mesh=mesh, in_specs=in_specs, out_specs=out_specs, check_vma=False)
```

```python
import functools
import math

import jax
import jax.numpy as jnp
from jax import lax
from jax.experimental import pallas as pl
from jax.experimental.pallas import tpu as pltpu
from jax.sharding import PartitionSpec as P

BLOCK = 128
ROUNDS = 2
UNROLL = 2
CHUNKS = 2
EPSILON = 1e-05

VMEM = pl.BlockSpec(memory_space=pltpu.VMEM)
SMEM = pl.BlockSpec(memory_space=pltpu.SMEM)
F32 = jnp.float32
BF16 = jnp.bfloat16


def dot(a, b):
    return jnp.dot(a, b, preferred_element_type=F32)


def params(mib=24):
    return pltpu.CompilerParams(vmem_limit_bytes=mib << 20)


def pieces(rows):
    return min(rows, 256)


def entry(slot, sender, taker, total):
    return slot + sender * 256 + taker * 65536 + total * 16777216


def list_length(slots):
    return slots + UNROLL


def spread_weights(labels, gains, index):
    marks = labels[...]
    weight = jnp.zeros(marks.shape, F32)
    for k in range(gains.shape[1]):
        weight = jnp.where(marks == k, gains[index, k], weight)
    return weight


def prepare_kernel(blocks, chunks, parity, gains, *refs):
    es, er, el, eo, ec, ms, mr, ml, mo, mc, ds, dr, dl, do, dc = refs[:15]
    e_list, m_list, d_list, counts, e_pick, m_pick, d_pick, e_put, m_put, d_put = refs[15:25]
    scratches = refs[25:]

    def finish(out, base, count):
        for k in range(UNROLL):
            out[base + count + k] = entry(0, 0, 0, blocks)
        return jnp.maximum((count + UNROLL - 1) // UNROLL, 1)

    def plain(sends, takes, live, out, where):
        total = live[0]

        def step(i, carry):
            taker = takes[i]
            out[i] = entry(i, sends[i], taker, taker)
            return carry

        lax.fori_loop(0, total, step, 0)
        counts[where] = finish(out, 0, total)

    plain(es, er, el, e_list, 0)
    plain(ds, dr, dl, d_list, 1)
    length = list_length(ms.shape[0])
    first = jnp.where(parity[0] == 0, 2, 0)
    per = blocks // chunks

    def step(i, carry):
        sender = ms[i]
        taker = mr[i]
        group = sender // blocks
        inner = sender - group * blocks
        part = inner // per
        local_sender = jnp.where(group == 1, inner, inner - part * per)
        which = jnp.where(
            group == 1, 0, jnp.where(group == first, 1 + part, 1 + chunks + part)
        )
        place = jnp.int32(0)
        for k in range(2 * chunks + 1):
            place = jnp.where(which == k, length * k + carry[k], place)
        m_list[place] = entry(i, local_sender, taker, taker)
        return tuple(c + (which == k).astype(jnp.int32) for k, c in enumerate(carry))

    zero = tuple(jnp.int32(0) for _ in range(2 * chunks + 1))
    found = lax.fori_loop(0, ml[0], step, zero)
    for k, count in enumerate(found):
        counts[2 + k] = finish(m_list, length * k, count)

    rows = lax.broadcasted_iota(jnp.int32, (BLOCK, BLOCK), 0)
    groups = ((ec, eo, e_pick, e_put), (mc, mo, m_pick, m_put), (dc, do, d_pick, d_put))
    for index, (labels, offsets, pick, put) in enumerate(groups):
        weights = scratches[index]
        weights[...] = spread_weights(labels, gains, index)

        def build(slot, carry, offsets=offsets, pick=pick, put=put, weights=weights):
            is_from = rows == offsets[pl.ds(2 * slot, 1), :]
            is_to = rows == offsets[pl.ds(2 * slot + 1, 1), :]
            both = jnp.concatenate(
                [jnp.where(is_from, 1.0, 0.0), jnp.where(is_to, 1.0, 0.0)], axis=0
            ).astype(BF16)
            where = pl.ds(pl.multiple_of(slot * BLOCK, BLOCK), BLOCK)
            pick[where, :] = both.T
            put[where, :] = jnp.where(is_to, weights[pl.ds(slot, 1), :], 0.0).astype(BF16)
            return carry

        lax.fori_loop(0, labels.shape[0], build, 0, unroll=4)


def prepare(blocks, chunks, parity, gains, enc, mesh, dec):
    i32 = jnp.int32
    sets = (enc, mesh, dec)
    slots = [s[0].shape[0] for s in sets]
    sizes = [list_length(slots[0]), (2 * chunks + 1) * list_length(slots[1])]
    sizes += [list_length(slots[2]), 8 + 2 * chunks]
    out_shape = [jax.ShapeDtypeStruct((n,), i32) for n in sizes]
    out_shape += [jax.ShapeDtypeStruct((n * BLOCK, 2 * BLOCK), BF16) for n in slots]
    out_shape += [jax.ShapeDtypeStruct((n * BLOCK, BLOCK), BF16) for n in slots]
    return pl.pallas_call(
        functools.partial(prepare_kernel, blocks, chunks),
        out_shape=out_shape,
        in_specs=[SMEM, SMEM] + [SMEM, SMEM, SMEM, VMEM, VMEM] * 3,
        out_specs=[SMEM] * 4 + [VMEM] * 6,
        scratch_shapes=[pltpu.VMEM((n, BLOCK), F32) for n in slots],
        compiler_params=params(20),
        cost_estimate=pl.CostEstimate(
            flops=2_000_000_000, bytes_accessed=13_000_000, transcendentals=0
        ),
    )(parity, gains, *enc, *mesh, *dec)


def edge_loop(base, trips, items, send, take, picks, puts, acc, held):
    def gather(i):
        for u in range(UNROLL):
            item = items[base + i * UNROLL + u]
            slot = pl.multiple_of((item & 255) * BLOCK, BLOCK)
            sender = pl.multiple_of(((item >> 8) & 255) * BLOCK, BLOCK)
            taker = pl.multiple_of(((item >> 16) & 255) * BLOCK, BLOCK)
            both = jnp.concatenate(
                [send[pl.ds(sender, BLOCK), :], take[pl.ds(taker, BLOCK), :]], axis=0
            )
            half = dot(picks[pl.ds(slot, BLOCK), :], both)
            held[u] = (half + half * jnp.tanh(half)).astype(BF16)

    def scatter(i):
        for u in range(UNROLL):
            item = items[base + i * UNROLL + u]
            slot = pl.multiple_of((item & 255) * BLOCK, BLOCK)
            total = pl.multiple_of((item >> 24) * BLOCK, BLOCK)
            acc[pl.ds(total, BLOCK), :] += dot(puts[pl.ds(slot, BLOCK), :], held[u])

    gather(0)

    def turn(i, carry):
        scatter(i - 1)
        gather(i)
        return carry

    lax.fori_loop(1, trips, turn, 0)
    scatter(trips - 1)


def edge_kernel(parts, first, last, counts, items, *refs):
    refs = list(refs)
    sends = [refs.pop(0) for _ in parts]
    take, picks, puts = refs[:3]
    refs = refs[3:]
    if not first:
        before = refs.pop(0)
    out = refs.pop(0)
    held = refs.pop(0)
    acc = refs.pop(0) if last else out
    if first:
        acc[...] = jnp.zeros_like(acc)
    elif last:
        acc[...] = before[...]
    for (where, base), send in zip(parts, sends):
        edge_loop(base, counts[where], items, send, take, picks, puts, acc, held)
    if last:
        out[...] = acc[pl.ds(0, out.shape[0]), :].astype(out.dtype)


def edge_sum(parts, counts, items, sends, take, picks, puts, before, last):
    first = before is None
    rows, columns = take.shape
    arrays = [counts, items, *sends, take, picks, puts]
    aliases = {}
    if not first:
        if not last:
            aliases = {len(arrays): 0}
        arrays.append(before)
    full = (rows + BLOCK, columns)
    scratch = [pltpu.VMEM((UNROLL, BLOCK, columns), BF16)]
    if last:
        scratch.append(pltpu.VMEM(full, F32))
        shape = jax.ShapeDtypeStruct((rows, columns), BF16)
    else:
        shape = jax.ShapeDtypeStruct(full, F32)
    return pl.pallas_call(
        functools.partial(edge_kernel, parts, first, last),
        out_shape=shape,
        in_specs=[SMEM, SMEM] + [VMEM] * (len(arrays) - 2),
        out_specs=VMEM,
        scratch_shapes=scratch,
        input_output_aliases=aliases,
        compiler_params=params(),
        cost_estimate=pl.CostEstimate(
            flops=2_000_000_000, bytes_accessed=2_000_000, transcendentals=1_000_000
        ),
    )(*arrays)


def two_dots(a, b, weights, mine, other, width):
    return dot(a, weights[pl.ds(mine, width), :]) + dot(b, weights[pl.ds(other, width), :])


def normalized(ym, yt):
    width = ym.shape[1] + yt.shape[1]
    total = jnp.sum(ym, axis=1, keepdims=True) + jnp.sum(yt, axis=1, keepdims=True)
    squares = jnp.sum(ym * ym, axis=1, keepdims=True) + jnp.sum(
        yt * yt, axis=1, keepdims=True
    )
    mean = total / width
    spread = squares / width - mean * mean
    return mean, lax.rsqrt(spread + EPSILON)


def mix_kernel(
    core, am, at, xm, xt, wm, wt, gm, gt, ws, out_m, out_t, out_s
):
    rows, width = am.shape
    tile = pieces(rows)
    mine = pl.multiple_of(core[0] * width, width)
    other = pl.multiple_of(width - core[0] * width, width)

    def step(t, carry):
        part = pl.ds(pl.multiple_of(t * tile, tile), tile)
        a = am[part, :]
        b = at[part, :]
        ym = two_dots(a, b, wm, mine, other, width)
        yt = two_dots(a, b, wt, mine, other, width)
        mean, scale = normalized(ym, yt)
        nm = (xm[part, :].astype(F32) + (ym - mean) * scale * gm[...]).astype(BF16)
        nt = (xt[part, :].astype(F32) + (yt - mean) * scale * gt[...]).astype(BF16)
        out_m[part, :] = nm
        out_t[part, :] = nt
        out_s[part, :] = (0.5 * two_dots(nm, nt, ws, mine, other, width)).astype(BF16)
        return carry

    lax.fori_loop(0, rows // tile, step, 0)


def mix(core, am, at, xm, xt, wm, wt, gm, gt, ws):
    shape = jax.ShapeDtypeStruct(am.shape, BF16)
    return pl.pallas_call(
        mix_kernel,
        out_shape=[shape] * 3,
        in_specs=[SMEM] + [VMEM] * 9,
        out_specs=[VMEM] * 3,
        compiler_params=params(),
    )(core, am, at, xm, xt, wm, wt, gm, gt, ws)


def project_kernel(core, xm, xt, w, bias, out):
    rows, width = xm.shape
    tile = pieces(rows)
    mine = pl.multiple_of(core[0] * width, width)
    other = pl.multiple_of(width - core[0] * width, width)

    def step(t, carry):
        part = pl.ds(pl.multiple_of(t * tile, tile), tile)
        y = two_dots(xm[part, :], xt[part, :], w, mine, other, width)
        out[part, :] = (0.5 * (y + bias[...])).astype(BF16)
        return carry

    lax.fori_loop(0, rows // tile, step, 0)


def project(core, xm, xt, w, bias):
    return pl.pallas_call(
        project_kernel,
        out_shape=jax.ShapeDtypeStruct(xm.shape, BF16),
        in_specs=[SMEM] + [VMEM] * 4,
        out_specs=VMEM,
        compiler_params=params(),
    )(core, xm, xt, w, bias)


def update_kernel(core, am, at, wm, wt, gm, out):
    rows, width = am.shape
    tile = pieces(rows)
    mine = pl.multiple_of(core[0] * width, width)
    other = pl.multiple_of(width - core[0] * width, width)

    def step(t, carry):
        part = pl.ds(pl.multiple_of(t * tile, tile), tile)
        a = am[part, :]
        b = at[part, :]
        ym = two_dots(a, b, wm, mine, other, width)
        yt = two_dots(a, b, wt, mine, other, width)
        mean, scale = normalized(ym, yt)
        out[part, :] = ((ym - mean) * scale * gm[...]).astype(BF16)
        return carry

    lax.fori_loop(0, rows // tile, step, 0)


def update_of(core, am, at, wm, wt, gm):
    return pl.pallas_call(
        update_kernel,
        out_shape=jax.ShapeDtypeStruct(am.shape, BF16),
        in_specs=[SMEM] + [VMEM] * 5,
        out_specs=VMEM,
        compiler_params=params(),
    )(core, am, at, wm, wt, gm)


def pick_rows_kernel(order, x, out):
    rows = x.shape[0]
    tile = pieces(rows)

    def step(t, carry):
        part = pl.ds(pl.multiple_of(t * tile, tile), tile)
        ids = lax.broadcasted_iota(jnp.int32, (rows, tile), 0)
        chosen = jnp.where(ids == order[:, part], 1.0, 0.0).astype(BF16)
        out[part, :] = lax.dot_general(
            chosen, x[...], (((0,), (0,)), ((), ())), preferred_element_type=F32
        ).astype(BF16)
        return carry

    lax.fori_loop(0, rows // tile, step, 0)


def pick_rows(order, x):
    return pl.pallas_call(
        pick_rows_kernel,
        out_shape=jax.ShapeDtypeStruct(x.shape, BF16),
        in_specs=[VMEM] * 2,
        out_specs=VMEM,
        compiler_params=params(),
    )(order, x)


def place_rows_kernel(order, x, rest, out):
    rows = x.shape[0]
    tile = pieces(rows)

    def step(t, carry):
        start = pl.multiple_of(t * tile, tile)
        part = pl.ds(start, tile)
        ids = lax.broadcasted_iota(jnp.int32, (tile, rows), 0) + start
        chosen = jnp.where(ids == order[...], 1.0, 0.0).astype(BF16)
        out[part, :] = (rest[part, :].astype(F32) + dot(chosen, x[...])).astype(BF16)
        return carry

    lax.fori_loop(0, rows // tile, step, 0)


def place_rows(order, x, rest):
    return pl.pallas_call(
        place_rows_kernel,
        out_shape=jax.ShapeDtypeStruct(x.shape, BF16),
        in_specs=[VMEM] * 3,
        out_specs=VMEM,
        compiler_params=params(),
    )(order, x, rest)


def swap(x):
    return lax.ppermute(x, "feat", [(0, 1), (1, 0)])


def exchange(x):
    return lax.all_to_all(x, "nodes", split_axis=0, concat_axis=0, tiled=True)


def tie(*values):
    return lax.optimization_barrier(values)


def ring(chunk, pairs):
    return lax.ppermute(chunk, "nodes", pairs)


def local(
    grid_latent,
    mesh_latent,
    grid_order,
    enc_send_block,
    enc_recv_block,
    enc_offsets,
    enc_classes,
    enc_live,
    mesh_send_block,
    mesh_recv_block,
    mesh_offsets,
    mesh_classes,
    mesh_live,
    dec_send_block,
    dec_recv_block,
    dec_offsets,
    dec_classes,
    dec_live,
    class_gain,
    enc_weights,
    mesh_weights,
    dec_weights,
    enc_bias,
    enc_gain,
    mesh_bias,
    mesh_gain,
    dec_bias,
    dec_gain,
):
    rows, columns = mesh_latent.shape
    size = lax.axis_size("nodes")
    to_near = [(j, j ^ 1) for j in range(size)]
    onward = [(j, (j + 2 - 4 * (j % 2)) % size) for j in range(size)]
    core = lax.axis_index("feat").astype(jnp.int32).reshape(1)
    parity = (lax.axis_index("nodes") % 2).astype(jnp.int32).reshape(1)
    arrived = exchange(pick_rows(grid_order, grid_latent))

    chunks = math.gcd(CHUNKS, rows // BLOCK)
    prepared = prepare(
        rows // BLOCK,
        chunks,
        parity,
        class_gain,
        (enc_send_block, enc_recv_block, enc_live, enc_offsets.reshape(-1, BLOCK), enc_classes),
        (mesh_send_block, mesh_recv_block, mesh_live, mesh_offsets.reshape(-1, BLOCK), mesh_classes),
        (dec_send_block, dec_recv_block, dec_live, dec_offsets.reshape(-1, BLOCK), dec_classes),
    )
    outs = [enc_weights[2], mesh_weights[0, 2], mesh_weights[1, 2], dec_weights[2]]
    outs_other = [swap(w) for w in outs]
    gains = jnp.stack([enc_gain, mesh_gain[0], mesh_gain[1]])
    gains_other = swap(gains)
    xm, xt = mesh_latent, swap(mesh_latent)
    take = project(core, xm, xt, enc_weights[1], enc_bias[None, :])
    arrived, prepared, take, outs, outs_other, gains, gains_other = tie(
        arrived, prepared, take, outs, outs_other, gains, gains_other
    )
    e_list, m_list, d_list, counts, e_pick, m_pick, d_pick, e_put, m_put, d_put = prepared
    length = list_length(mesh_send_block.shape[0])

    arrived_other = swap(arrived)
    nothing = jnp.zeros((1, columns), F32)
    send = project(core, arrived, arrived_other, enc_weights[0], nothing)
    agg = edge_sum(((0, 0),), counts, e_list, [send], take, e_pick, e_put, None, True)
    grid_take = project(core, arrived, arrived_other, dec_weights[1], dec_bias[None, :])
    for r in range(ROUNDS):
        xm, xt, send = mix(
            core,
            agg,
            swap(agg),
            xm,
            xt,
            outs[r],
            outs_other[r],
            gains[r : r + 1],
            gains_other[r : r + 1],
            mesh_weights[r, 0],
        )
        near = [ring(x, to_near) for x in jnp.split(send, chunks)]
        take = project(core, xm, xt, mesh_weights[r, 1], mesh_bias[r][None, :])
        total = edge_sum(
            ((2, 0),), counts, m_list, [send], take, m_pick, m_put, None, False
        )
        far = []
        for k in range(chunks):
            near[k], total = tie(near[k], total)
            far.append(ring(near[k], onward))
        parts = [(3 + k, length * (1 + k)) for k in range(2 * chunks)]
        total = edge_sum(
            tuple(parts[:chunks]), counts, m_list, near, take, m_pick, m_put, total, False
        )
        if chunks > 1:
            total = edge_sum(
                tuple(parts[chunks:-1]),
                counts,
                m_list,
                far[:-1],
                take,
                m_pick,
                m_put,
                total,
                False,
            )
        agg = edge_sum(
            tuple(parts[-1:]), counts, m_list, far[-1:], take, m_pick, m_put, total, True
        )
    xm, xt, send = mix(
        core,
        agg,
        swap(agg),
        xm,
        xt,
        outs[ROUNDS],
        outs_other[ROUNDS],
        gains[ROUNDS : ROUNDS + 1],
        gains_other[ROUNDS : ROUNDS + 1],
        dec_weights[0],
    )
    agg = edge_sum(((1, 0),), counts, d_list, [send], grid_take, d_pick, d_put, None, True)
    update = update_of(
        core, agg, swap(agg), outs[3], outs_other[3], dec_gain[None, :]
    )
    grid_out = place_rows(grid_order, exchange(update), grid_latent)
    return grid_out, xm


def solution(mesh):
    in_specs = (
        P("nodes", "feat"),
        P("nodes", "feat"),
        P("nodes", None),
        P("nodes"),
        P("nodes"),
        P("nodes", None, None),
        P("nodes", None),
        P("nodes"),
        P("nodes"),
        P("nodes"),
        P("nodes", None, None),
        P("nodes", None),
        P("nodes"),
        P("nodes"),
        P("nodes"),
        P("nodes", None, None),
        P("nodes", None),
        P("nodes"),
        P(),
        P(None, None, "feat"),
        P(None, None, None, "feat"),
        P(None, None, "feat"),
        P("feat"),
        P("feat"),
        P(None, "feat"),
        P(None, "feat"),
        P("feat"),
        P("feat"),
    )
    out_specs = (P("nodes", "feat"), P("nodes", "feat"))
    return jax.shard_map(local, mesh=mesh, in_specs=in_specs, out_specs=out_specs, check_vma=False)
```

```python
import functools
import math

import jax
import jax.numpy as jnp
from jax import lax
from jax.experimental import pallas as pl
from jax.experimental.pallas import tpu as pltpu
from jax.sharding import PartitionSpec as P

BLOCK = 128
ROUNDS = 2
UNROLL = 2
CHUNKS = 2
EPSILON = 1e-05

VMEM = pl.BlockSpec(memory_space=pltpu.VMEM)
SMEM = pl.BlockSpec(memory_space=pltpu.SMEM)
F32 = jnp.float32
BF16 = jnp.bfloat16


def dot(a, b):
    return jnp.dot(a, b, preferred_element_type=F32)


def params(mib=24):
    return pltpu.CompilerParams(vmem_limit_bytes=mib << 20)


def pieces(rows):
    return min(rows, 256)


def entry(slot, sender, taker, total):
    return slot + sender * 256 + taker * 65536 + total * 16777216


def list_length(slots):
    return slots + UNROLL


def spread_weights(labels, gains, index):
    marks = labels[...]
    weight = jnp.zeros(marks.shape, F32)
    for k in range(gains.shape[1]):
        weight = jnp.where(marks == k, gains[index, k], weight)
    return weight


def prepare_kernel(blocks, chunks, parity, *refs):
    inputs, refs = refs[:13], refs[13:]
    (e_list, m_list, d_list, counts, e_w, m_w, d_w), refs = refs[:7], refs[7:]
    held, sems = refs[:13], refs[13]
    copies = [
        pltpu.make_async_copy(source, target, sems.at[k])
        for k, (source, target) in enumerate(zip(inputs, held))
    ]
    for copy in copies:
        copy.start()
    for copy in copies:
        copy.wait()
    gains, es, er, el, ec, ms, mr, ml, mc, ds, dr, dl, dc = held

    def finish(out, base, count):
        for k in range(UNROLL):
            out[base + count + k] = entry(0, 0, 0, blocks)
        return jnp.maximum((count + UNROLL - 1) // UNROLL, 1)

    def plain(sends, takes, live, out, where):
        total = live[0]

        def step(i, carry):
            taker = takes[i]
            out[i] = entry(i, sends[i], taker, taker)
            return carry

        lax.fori_loop(0, total, step, 0)
        counts[where] = finish(out, 0, total)

    plain(es, er, el, e_list, 0)
    plain(ds, dr, dl, d_list, 1)
    length = list_length(ms.shape[0])
    first = jnp.where(parity[0] == 0, 2, 0)
    per = blocks // chunks

    def step(i, carry):
        sender = ms[i]
        taker = mr[i]
        group = sender // blocks
        inner = sender - group * blocks
        part = inner // per
        local_sender = jnp.where(group == 1, inner, inner - part * per)
        which = jnp.where(
            group == 1, 0, jnp.where(group == first, 1 + part, 1 + chunks + part)
        )
        place = jnp.int32(0)
        for k in range(2 * chunks + 1):
            place = jnp.where(which == k, length * k + carry[k], place)
        m_list[place] = entry(i, local_sender, taker, taker)
        return tuple(c + (which == k).astype(jnp.int32) for k, c in enumerate(carry))

    zero = tuple(jnp.int32(0) for _ in range(2 * chunks + 1))
    found = lax.fori_loop(0, ml[0], step, zero)
    for k, count in enumerate(found):
        counts[2 + k] = finish(m_list, length * k, count)

    for index, (labels, out) in enumerate(((ec, e_w), (mc, m_w), (dc, d_w))):
        out[...] = spread_weights(labels, gains, index)


def prepare(blocks, chunks, parity, gains, enc, mesh, dec):
    i32 = jnp.int32
    sets = (enc, mesh, dec)
    slots = [s[0].shape[0] for s in sets]
    sizes = [list_length(slots[0]), (2 * chunks + 1) * list_length(slots[1])]
    sizes += [list_length(slots[2]), 8 + 2 * chunks]
    out_shape = [jax.ShapeDtypeStruct((n,), i32) for n in sizes]
    out_shape += [jax.ShapeDtypeStruct((n, BLOCK), F32) for n in slots]
    arrays = [gains, *enc, *mesh, *dec]
    spaces = [pltpu.SMEM] + [pltpu.SMEM, pltpu.SMEM, pltpu.SMEM, pltpu.VMEM] * 3
    scratch = [space(x.shape, x.dtype) for space, x in zip(spaces, arrays)]
    scratch.append(pltpu.SemaphoreType.DMA((len(arrays),)))
    return pl.pallas_call(
        functools.partial(prepare_kernel, blocks, chunks),
        out_shape=out_shape,
        in_specs=[SMEM] + [pl.BlockSpec(memory_space=pl.ANY)] * len(arrays),
        out_specs=[SMEM] * 4 + [VMEM] * 3,
        scratch_shapes=scratch,
        compiler_params=params(4),
        cost_estimate=pl.CostEstimate(
            flops=2_000_000_000, bytes_accessed=1_000_000, transcendentals=0
        ),
    )(parity, *arrays)


def edge_loop(base, trips, items, send, take, offsets, weights, acc, picks, puts, held):
    rows = lax.broadcasted_iota(jnp.int32, (BLOCK, BLOCK), 0).astype(F32).astype(BF16)
    one = jnp.ones((BLOCK, BLOCK), BF16)
    nil = jnp.zeros((BLOCK, BLOCK), BF16)

    def spread(row):
        return jnp.broadcast_to(row.astype(F32).astype(BF16), (BLOCK, BLOCK))

    def build(i):
        for u in range(UNROLL):
            slot = items[base + i * UNROLL + u] & 255
            is_from = rows == spread(offsets[pl.ds(2 * slot, 1), :])
            is_to = rows == spread(offsets[pl.ds(2 * slot + 1, 1), :])
            both = [jnp.where(is_from, one, nil), jnp.where(is_to, one, nil)]
            picks[u] = jnp.concatenate([x.T for x in both], axis=1)
            puts[u] = jnp.where(is_to, spread(weights[pl.ds(slot, 1), :]), nil)

    def gather(i):
        for u in range(UNROLL):
            item = items[base + i * UNROLL + u]
            sender = pl.multiple_of(((item >> 8) & 255) * BLOCK, BLOCK)
            taker = pl.multiple_of(((item >> 16) & 255) * BLOCK, BLOCK)
            both = jnp.concatenate(
                [send[pl.ds(sender, BLOCK), :], take[pl.ds(taker, BLOCK), :]], axis=0
            )
            half = dot(picks[u], both)
            held[u] = (half + half * jnp.tanh(half)).astype(BF16)

    def scatter(i):
        for u in range(UNROLL):
            item = items[base + i * UNROLL + u]
            total = pl.multiple_of((item >> 24) * BLOCK, BLOCK)
            acc[pl.ds(total, BLOCK), :] += dot(puts[u], held[u])

    def turn(i, carry):
        scatter(i - 1)
        build(i)
        gather(i)
        return carry

    build(0)
    gather(0)
    lax.fori_loop(1, trips, turn, 0)
    scatter(trips - 1)


def edge_kernel(parts, first, last, counts, items, *refs):
    refs = list(refs)
    sends = [refs.pop(0) for _ in parts]
    take, offsets, weights = refs[:3]
    refs = refs[3:]
    if not first:
        before = refs.pop(0)
    out = refs.pop(0)
    spare = [refs.pop(0) for _ in range(3)]
    acc = refs.pop(0) if last else out
    if first:
        acc[...] = jnp.zeros_like(acc)
    elif last:
        acc[...] = before[...]
    for (where, base), send in zip(parts, sends):
        edge_loop(base, counts[where], items, send, take, offsets, weights, acc, *spare)
    if last:
        out[...] = acc[pl.ds(0, out.shape[0]), :].astype(out.dtype)


def edge_sum(parts, counts, items, sends, take, offsets, weights, before, last):
    first = before is None
    rows, columns = take.shape
    arrays = [counts, items, *sends, take, offsets, weights]
    aliases = {}
    if not first:
        if not last:
            aliases = {len(arrays): 0}
        arrays.append(before)
    full = (rows + BLOCK, columns)
    scratch = [
        pltpu.VMEM((UNROLL, BLOCK, width), BF16) for width in (2 * BLOCK, BLOCK, columns)
    ]
    if last:
        scratch.append(pltpu.VMEM(full, F32))
        shape = jax.ShapeDtypeStruct((rows, columns), BF16)
    else:
        shape = jax.ShapeDtypeStruct(full, F32)
    return pl.pallas_call(
        functools.partial(edge_kernel, parts, first, last),
        out_shape=shape,
        in_specs=[SMEM, SMEM] + [VMEM] * (len(arrays) - 2),
        out_specs=VMEM,
        scratch_shapes=scratch,
        input_output_aliases=aliases,
        compiler_params=params(),
        cost_estimate=pl.CostEstimate(
            flops=2_000_000_000, bytes_accessed=2_000_000, transcendentals=1_000_000
        ),
    )(*arrays)


def two_dots(a, b, weights, mine, other, width):
    return dot(a, weights[pl.ds(mine, width), :]) + dot(b, weights[pl.ds(other, width), :])


def normalized(ym, yt):
    width = ym.shape[1] + yt.shape[1]
    total = jnp.sum(ym, axis=1, keepdims=True) + jnp.sum(yt, axis=1, keepdims=True)
    squares = jnp.sum(ym * ym, axis=1, keepdims=True) + jnp.sum(
        yt * yt, axis=1, keepdims=True
    )
    mean = total / width
    spread = squares / width - mean * mean
    return mean, lax.rsqrt(spread + EPSILON)


def mix_kernel(
    core, am, at, xm, xt, wm, wt, gm, gt, ws, out_m, out_t, out_s
):
    rows, width = am.shape
    tile = pieces(rows)
    mine = pl.multiple_of(core[0] * width, width)
    other = pl.multiple_of(width - core[0] * width, width)

    def step(t, carry):
        part = pl.ds(pl.multiple_of(t * tile, tile), tile)
        a = am[part, :]
        b = at[part, :]
        ym = two_dots(a, b, wm, mine, other, width)
        yt = two_dots(a, b, wt, mine, other, width)
        mean, scale = normalized(ym, yt)
        nm = (xm[part, :].astype(F32) + (ym - mean) * scale * gm[...]).astype(BF16)
        nt = (xt[part, :].astype(F32) + (yt - mean) * scale * gt[...]).astype(BF16)
        out_m[part, :] = nm
        out_t[part, :] = nt
        out_s[part, :] = (0.5 * two_dots(nm, nt, ws, mine, other, width)).astype(BF16)
        return carry

    lax.fori_loop(0, rows // tile, step, 0)


def mix(core, am, at, xm, xt, wm, wt, gm, gt, ws):
    shape = jax.ShapeDtypeStruct(am.shape, BF16)
    return pl.pallas_call(
        mix_kernel,
        out_shape=[shape] * 3,
        in_specs=[SMEM] + [VMEM] * 9,
        out_specs=[VMEM] * 3,
        compiler_params=params(),
    )(core, am, at, xm, xt, wm, wt, gm, gt, ws)


def project_kernel(core, xm, xt, w, bias, out):
    rows, width = xm.shape
    tile = pieces(rows)
    mine = pl.multiple_of(core[0] * width, width)
    other = pl.multiple_of(width - core[0] * width, width)

    def step(t, carry):
        part = pl.ds(pl.multiple_of(t * tile, tile), tile)
        y = two_dots(xm[part, :], xt[part, :], w, mine, other, width)
        out[part, :] = (0.5 * (y + bias[...])).astype(BF16)
        return carry

    lax.fori_loop(0, rows // tile, step, 0)


def project(core, xm, xt, w, bias):
    return pl.pallas_call(
        project_kernel,
        out_shape=jax.ShapeDtypeStruct(xm.shape, BF16),
        in_specs=[SMEM] + [VMEM] * 4,
        out_specs=VMEM,
        compiler_params=params(),
    )(core, xm, xt, w, bias)


def update_kernel(core, am, at, wm, wt, gm, out):
    rows, width = am.shape
    tile = pieces(rows)
    mine = pl.multiple_of(core[0] * width, width)
    other = pl.multiple_of(width - core[0] * width, width)

    def step(t, carry):
        part = pl.ds(pl.multiple_of(t * tile, tile), tile)
        a = am[part, :]
        b = at[part, :]
        ym = two_dots(a, b, wm, mine, other, width)
        yt = two_dots(a, b, wt, mine, other, width)
        mean, scale = normalized(ym, yt)
        out[part, :] = ((ym - mean) * scale * gm[...]).astype(BF16)
        return carry

    lax.fori_loop(0, rows // tile, step, 0)


def update_of(core, am, at, wm, wt, gm):
    return pl.pallas_call(
        update_kernel,
        out_shape=jax.ShapeDtypeStruct(am.shape, BF16),
        in_specs=[SMEM] + [VMEM] * 5,
        out_specs=VMEM,
        compiler_params=params(),
    )(core, am, at, wm, wt, gm)


def pick_rows_kernel(order, x, out):
    rows = x.shape[0]
    tile = pieces(rows)

    def step(t, carry):
        part = pl.ds(pl.multiple_of(t * tile, tile), tile)
        ids = lax.broadcasted_iota(jnp.int32, (rows, tile), 0)
        chosen = jnp.where(ids == order[:, part], 1.0, 0.0).astype(BF16)
        out[part, :] = lax.dot_general(
            chosen, x[...], (((0,), (0,)), ((), ())), preferred_element_type=F32
        ).astype(BF16)
        return carry

    lax.fori_loop(0, rows // tile, step, 0)


def pick_rows(order, x):
    return pl.pallas_call(
        pick_rows_kernel,
        out_shape=jax.ShapeDtypeStruct(x.shape, BF16),
        in_specs=[VMEM] * 2,
        out_specs=VMEM,
        compiler_params=params(),
    )(order, x)


def place_rows_kernel(order, x, rest, out):
    rows = x.shape[0]
    tile = pieces(rows)

    def step(t, carry):
        start = pl.multiple_of(t * tile, tile)
        part = pl.ds(start, tile)
        ids = lax.broadcasted_iota(jnp.int32, (tile, rows), 0) + start
        chosen = jnp.where(ids == order[...], 1.0, 0.0).astype(BF16)
        out[part, :] = (rest[part, :].astype(F32) + dot(chosen, x[...])).astype(BF16)
        return carry

    lax.fori_loop(0, rows // tile, step, 0)


def place_rows(order, x, rest):
    return pl.pallas_call(
        place_rows_kernel,
        out_shape=jax.ShapeDtypeStruct(x.shape, BF16),
        in_specs=[VMEM] * 3,
        out_specs=VMEM,
        compiler_params=params(),
    )(order, x, rest)


def swap(x):
    return lax.ppermute(x, "feat", [(0, 1), (1, 0)])


def exchange(x):
    return lax.all_to_all(x, "nodes", split_axis=0, concat_axis=0, tiled=True)


def tie(*values):
    return lax.optimization_barrier(values)


def ring(chunk, pairs):
    return lax.ppermute(chunk, "nodes", pairs)


def local(
    grid_latent,
    mesh_latent,
    grid_order,
    enc_send_block,
    enc_recv_block,
    enc_offsets,
    enc_classes,
    enc_live,
    mesh_send_block,
    mesh_recv_block,
    mesh_offsets,
    mesh_classes,
    mesh_live,
    dec_send_block,
    dec_recv_block,
    dec_offsets,
    dec_classes,
    dec_live,
    class_gain,
    enc_weights,
    mesh_weights,
    dec_weights,
    enc_bias,
    enc_gain,
    mesh_bias,
    mesh_gain,
    dec_bias,
    dec_gain,
):
    rows, columns = mesh_latent.shape
    size = lax.axis_size("nodes")
    to_near = [(j, j ^ 1) for j in range(size)]
    onward = [(j, (j + 2 - 4 * (j % 2)) % size) for j in range(size)]
    core = lax.axis_index("feat").astype(jnp.int32).reshape(1)
    parity = (lax.axis_index("nodes") % 2).astype(jnp.int32).reshape(1)
    arrived = exchange(pick_rows(grid_order, grid_latent))

    chunks = math.gcd(CHUNKS, rows // BLOCK)
    prepared = prepare(
        rows // BLOCK,
        chunks,
        parity,
        class_gain,
        (enc_send_block, enc_recv_block, enc_live, enc_classes),
        (mesh_send_block, mesh_recv_block, mesh_live, mesh_classes),
        (dec_send_block, dec_recv_block, dec_live, dec_classes),
    )
    e_off = enc_offsets.reshape(-1, BLOCK)
    m_off = mesh_offsets.reshape(-1, BLOCK)
    d_off = dec_offsets.reshape(-1, BLOCK)
    outs = [enc_weights[2], mesh_weights[0, 2], mesh_weights[1, 2], dec_weights[2]]
    outs_other = [swap(outs[0])]
    gains = [enc_gain[None, :], mesh_gain]
    gains_other = [swap(x) for x in gains]
    xm, xt = mesh_latent, swap(mesh_latent)
    take = project(core, xm, xt, enc_weights[1], enc_bias[None, :])
    arrived, prepared, take, outs_other, gains_other = tie(
        arrived, prepared, take, outs_other, gains_other
    )
    gains = [gains[0], gains[1][:1], gains[1][1:]]
    gains_other = [gains_other[0], gains_other[1][:1], gains_other[1][1:]]
    e_list, m_list, d_list, counts, e_w, m_w, d_w = prepared
    length = list_length(mesh_send_block.shape[0])

    arrived_other = swap(arrived)
    nothing = jnp.zeros((1, columns), F32)
    send = project(core, arrived, arrived_other, enc_weights[0], nothing)
    agg = edge_sum(((0, 0),), counts, e_list, [send], take, e_off, e_w, None, True)
    grid_take = project(core, arrived, arrived_other, dec_weights[1], dec_bias[None, :])
    for r in range(ROUNDS):
        xm, xt, send = mix(
            core,
            agg,
            swap(agg),
            xm,
            xt,
            outs[r],
            outs_other[r],
            gains[r],
            gains_other[r],
            mesh_weights[r, 0],
        )
        near = [ring(x, to_near) for x in jnp.split(send, chunks)]
        take = project(core, xm, xt, mesh_weights[r, 1], mesh_bias[r][None, :])
        total = edge_sum(
            ((2, 0),), counts, m_list, [send], take, m_off, m_w, None, False
        )
        fresh = outs[r + 1 : r + 2] if r + 1 < ROUNDS else outs[r + 1 :]
        fresh, total = tie(fresh, total)
        fresh = [swap(w) for w in fresh]
        far = []
        for k in range(chunks):
            near[k], total = tie(near[k], total)
            far.append(ring(near[k], onward))
        parts = [(3 + k, length * (1 + k)) for k in range(2 * chunks)]
        total = edge_sum(
            tuple(parts[:chunks]), counts, m_list, near, take, m_off, m_w, total, False
        )
        total, fresh = tie(total, fresh)
        outs_other += fresh
        if chunks > 1:
            total = edge_sum(
                tuple(parts[chunks:-1]),
                counts,
                m_list,
                far[:-1],
                take,
                m_off,
                m_w,
                total,
                False,
            )
        agg = edge_sum(
            tuple(parts[-1:]), counts, m_list, far[-1:], take, m_off, m_w, total, True
        )
    xm, xt, send = mix(
        core,
        agg,
        swap(agg),
        xm,
        xt,
        outs[ROUNDS],
        outs_other[ROUNDS],
        gains[ROUNDS],
        gains_other[ROUNDS],
        dec_weights[0],
    )
    agg = edge_sum(((1, 0),), counts, d_list, [send], grid_take, d_off, d_w, None, True)
    update = update_of(
        core, agg, swap(agg), outs[3], outs_other[3], dec_gain[None, :]
    )
    grid_out = place_rows(grid_order, exchange(update), grid_latent)
    return grid_out, xm


def solution(mesh):
    in_specs = (
        P("nodes", "feat"),
        P("nodes", "feat"),
        P("nodes", None),
        P("nodes"),
        P("nodes"),
        P("nodes", None, None),
        P("nodes", None),
        P("nodes"),
        P("nodes"),
        P("nodes"),
        P("nodes", None, None),
        P("nodes", None),
        P("nodes"),
        P("nodes"),
        P("nodes"),
        P("nodes", None, None),
        P("nodes", None),
        P("nodes"),
        P(),
        P(None, None, "feat"),
        P(None, None, None, "feat"),
        P(None, None, "feat"),
        P("feat"),
        P("feat"),
        P(None, "feat"),
        P(None, "feat"),
        P("feat"),
        P("feat"),
    )
    out_specs = (P("nodes", "feat"), P("nodes", "feat"))
    return jax.shard_map(local, mesh=mesh, in_specs=in_specs, out_specs=out_specs, check_vma=False)
```

```python
import functools
import math

import jax
import jax.numpy as jnp
from jax import lax
from jax.experimental import pallas as pl
from jax.experimental.pallas import tpu as pltpu
from jax.sharding import PartitionSpec as P

BLOCK = 128
ROUNDS = 2
UNROLL = 4
CHUNKS = 4
EPSILON = 1e-05

VMEM = pl.BlockSpec(memory_space=pltpu.VMEM)
SMEM = pl.BlockSpec(memory_space=pltpu.SMEM)
HBM = pl.BlockSpec(memory_space=pltpu.HBM)
F32 = jnp.float32
BF16 = jnp.bfloat16


def dot(a, b):
    return jnp.dot(a, b, preferred_element_type=F32)


def params(mib=24):
    return pltpu.CompilerParams(vmem_limit_bytes=mib << 20)


def pieces(rows):
    return min(rows, 256)


def entry(slot, sender, taker, total):
    return slot + sender * 256 + taker * 65536 + total * 16777216


def list_length(slots):
    return slots + 2 * UNROLL


def spread_weights(labels, gains, index):
    marks = labels[...]
    weight = jnp.zeros(marks.shape, F32)
    for k in range(gains.shape[1]):
        weight = jnp.where(marks == k, gains[index, k], weight)
    return weight


def prepare_kernel(blocks, chunks, parity, *refs):
    inputs, refs = refs[:13], refs[13:]
    (e_list, m_list, d_list, counts, e_w, m_w, d_w), refs = refs[:7], refs[7:]
    held, sems = refs[:13], refs[13]
    copies = [
        pltpu.make_async_copy(source, target, sems.at[k])
        for k, (source, target) in enumerate(zip(inputs, held))
    ]
    for copy in copies:
        copy.start()
    for copy in copies:
        copy.wait()
    gains, es, er, el, ec, ms, mr, ml, mc, ds, dr, dl, dc = held

    def finish(out, base, count):
        for k in range(2 * UNROLL):
            out[base + count + k] = entry(0, 0, 0, blocks)
        return jnp.maximum((count + UNROLL - 1) // UNROLL, 1)

    def plain(sends, takes, live, out, where):
        total = live[0]

        def step(i, carry):
            taker = takes[i]
            out[i] = entry(i, sends[i], taker, taker)
            return carry

        lax.fori_loop(0, total, step, 0)
        counts[where] = finish(out, 0, total)

    plain(es, er, el, e_list, 0)
    plain(ds, dr, dl, d_list, 1)
    length = list_length(ms.shape[0])
    first = jnp.where(parity[0] == 0, 2, 0)
    last = 2 - first
    per = blocks // chunks

    def step(i, carry):
        sender = ms[i]
        taker = mr[i]
        group = sender // blocks
        inner = sender - group * blocks
        late = inner >= blocks - per
        inner = jnp.where((group == last) & late, inner - (blocks - per), inner)
        which = jnp.where(
            group == 1, 0, jnp.where(group == first, 1, jnp.where(late, 3, 2))
        )
        place = carry[0]
        for k in range(1, 4):
            place = jnp.where(which == k, length * k + carry[k], place)
        m_list[place] = entry(i, inner, taker, taker)
        return tuple(c + (which == k).astype(jnp.int32) for k, c in enumerate(carry))

    zero = tuple(jnp.int32(0) for _ in range(4))
    found = lax.fori_loop(0, ml[0], step, zero)
    for k, count in enumerate(found):
        counts[2 + k] = finish(m_list, length * k, count)

    for index, (labels, out) in enumerate(((ec, e_w), (mc, m_w), (dc, d_w))):
        out[...] = spread_weights(labels, gains, index)


def prepare(blocks, chunks, parity, gains, enc, mesh, dec):
    i32 = jnp.int32
    sets = (enc, mesh, dec)
    slots = [s[0].shape[0] for s in sets]
    sizes = [list_length(slots[0]), 4 * list_length(slots[1])]
    sizes += [list_length(slots[2]), 8]
    out_shape = [jax.ShapeDtypeStruct((n,), i32) for n in sizes]
    out_shape += [jax.ShapeDtypeStruct((n, BLOCK), F32) for n in slots]
    arrays = [gains, *enc, *mesh, *dec]
    spaces = [pltpu.SMEM] + [pltpu.SMEM, pltpu.SMEM, pltpu.SMEM, pltpu.VMEM] * 3
    scratch = [space(x.shape, x.dtype) for space, x in zip(spaces, arrays)]
    scratch.append(pltpu.SemaphoreType.DMA((len(arrays),)))
    return pl.pallas_call(
        functools.partial(prepare_kernel, blocks, chunks),
        out_shape=out_shape,
        in_specs=[SMEM] + [HBM] * len(arrays),
        out_specs=[SMEM] * 4 + [VMEM] * 3,
        scratch_shapes=scratch,
        compiler_params=params(4),
        cost_estimate=pl.CostEstimate(
            flops=2_000_000_000, bytes_accessed=1_000_000, transcendentals=0
        ),
    )(parity, *arrays)


def edge_loop(base, trips, items, send, take, offsets, weights, acc, picks, held):
    rows = lax.broadcasted_iota(jnp.int32, (BLOCK, BLOCK), 0).astype(F32).astype(BF16)
    one = jnp.ones((BLOCK, BLOCK), BF16)
    nil = jnp.zeros((BLOCK, BLOCK), BF16)

    def spread(row):
        return jnp.broadcast_to(row.astype(F32).astype(BF16), (BLOCK, BLOCK))

    def build(i):
        for u in range(UNROLL):
            slot = items[base + i * UNROLL + u] & 255
            both = [
                jnp.where(rows == spread(offsets[pl.ds(2 * slot + k, 1), :]), one, nil)
                for k in range(2)
            ]
            picks[u] = jnp.concatenate([x.T for x in both], axis=1)

    def gather(i):
        for u in range(UNROLL):
            item = items[base + i * UNROLL + u]
            sender = pl.multiple_of(((item >> 8) & 255) * BLOCK, BLOCK)
            taker = pl.multiple_of(((item >> 16) & 255) * BLOCK, BLOCK)
            both = jnp.concatenate(
                [send[pl.ds(sender, BLOCK), :], take[pl.ds(taker, BLOCK), :]], axis=0
            )
            half = dot(picks[u], both)
            held[u] = (half + half * jnp.tanh(half)).astype(BF16)

    def scatter(i):
        for u in range(UNROLL):
            item = items[base + i * UNROLL + u]
            slot = item & 255
            total = pl.multiple_of((item >> 24) * BLOCK, BLOCK)
            is_to = rows == spread(offsets[pl.ds(2 * slot + 1, 1), :])
            put = jnp.where(is_to, spread(weights[pl.ds(slot, 1), :]), nil)
            acc[pl.ds(total, BLOCK), :] += dot(put, held[u])

    def turn(i, carry):
        scatter(i - 1)
        gather(i)
        build(i + 1)
        return carry

    build(0)
    gather(0)
    build(1)
    lax.fori_loop(1, trips, turn, 0)
    scatter(trips - 1)


def edge_kernel(where, base, pieces_in, first, last, counts, items, *refs):
    refs = list(refs)
    sends = [refs.pop(0) for _ in range(pieces_in)]
    take, offsets, weights = refs[:3]
    refs = refs[3:]
    if not first:
        before = refs.pop(0)
    out, picks, held = refs[:3]
    refs = refs[3:]
    acc = refs.pop(0) if last else out
    if first:
        acc[...] = jnp.zeros_like(acc)
    elif last:
        acc[...] = before[...]
    send = sends[0]
    if pieces_in > 1:
        joined = refs.pop(0)
        depth = send.shape[0]
        for k, piece in enumerate(sends):
            joined[pl.ds(k * depth, depth), :] = piece[...]
        send = joined
    edge_loop(base, counts[where], items, send, take, offsets, weights, acc, picks, held)
    if last:
        out[...] = acc[pl.ds(0, out.shape[0]), :].astype(out.dtype)


def edge_sum(where, base, counts, items, sends, take, offsets, weights, before, last):
    first = before is None
    rows, columns = take.shape
    arrays = [counts, items, *sends, take, offsets, weights]
    aliases = {}
    if not first:
        if not last:
            aliases = {len(arrays): 0}
        arrays.append(before)
    full = (rows + BLOCK, columns)
    scratch = [
        pltpu.VMEM((UNROLL, BLOCK, width), BF16) for width in (2 * BLOCK, columns)
    ]
    if last:
        scratch.append(pltpu.VMEM(full, F32))
        shape = jax.ShapeDtypeStruct((rows, columns), BF16)
    else:
        shape = jax.ShapeDtypeStruct(full, F32)
    if len(sends) > 1:
        depth = sum(x.shape[0] for x in sends)
        scratch.append(pltpu.VMEM((depth, columns), BF16))
    return pl.pallas_call(
        functools.partial(edge_kernel, where, base, len(sends), first, last),
        out_shape=shape,
        in_specs=[SMEM, SMEM] + [VMEM] * (len(arrays) - 2),
        out_specs=VMEM,
        scratch_shapes=scratch,
        input_output_aliases=aliases,
        compiler_params=params(),
        cost_estimate=pl.CostEstimate(
            flops=2_000_000_000, bytes_accessed=2_000_000, transcendentals=1_000_000
        ),
    )(*arrays)


def two_dots(a, b, weights, mine, other, width):
    return dot(a, weights[pl.ds(mine, width), :]) + dot(b, weights[pl.ds(other, width), :])


def normalized(ym, yt):
    width = ym.shape[1] + yt.shape[1]
    total = jnp.sum(ym + yt, axis=1, keepdims=True)
    squares = jnp.sum(ym * ym + yt * yt, axis=1, keepdims=True)
    mean = total / width
    spread = squares / width - mean * mean
    return mean, lax.rsqrt(spread + EPSILON)


def mix_kernel(
    core, am, at, xm, xt, wm, wt, gm, gt, ws, out_m, out_t, out_s
):
    rows, width = am.shape
    tile = pieces(rows)
    mine = pl.multiple_of(core[0] * width, width)
    other = pl.multiple_of(width - core[0] * width, width)

    for t in range(rows // tile):
        part = pl.ds(t * tile, tile)
        a = am[part, :]
        b = at[part, :]
        ym = two_dots(a, b, wm, mine, other, width)
        yt = two_dots(a, b, wt, mine, other, width)
        mean, scale = normalized(ym, yt)
        nm = (xm[part, :].astype(F32) + (ym - mean) * scale * gm[...]).astype(BF16)
        nt = (xt[part, :].astype(F32) + (yt - mean) * scale * gt[...]).astype(BF16)
        out_m[part, :] = nm
        out_t[part, :] = nt
        out_s[part, :] = (0.5 * two_dots(nm, nt, ws, mine, other, width)).astype(BF16)


def mix(core, am, at, xm, xt, wm, wt, gm, gt, ws):
    shape = jax.ShapeDtypeStruct(am.shape, BF16)
    return pl.pallas_call(
        mix_kernel,
        out_shape=[shape] * 3,
        in_specs=[SMEM] + [VMEM] * 9,
        out_specs=[VMEM] * 3,
        compiler_params=params(),
    )(core, am, at, xm, xt, wm, wt, gm, gt, ws)


def project_kernel(core, xm, xt, w, bias, out):
    rows, width = xm.shape
    tile = pieces(rows)
    mine = pl.multiple_of(core[0] * width, width)
    other = pl.multiple_of(width - core[0] * width, width)

    for t in range(rows // tile):
        part = pl.ds(t * tile, tile)
        y = two_dots(xm[part, :], xt[part, :], w, mine, other, width)
        out[part, :] = (0.5 * (y + bias[...])).astype(BF16)


def project(core, xm, xt, w, bias):
    return pl.pallas_call(
        project_kernel,
        out_shape=jax.ShapeDtypeStruct(xm.shape, BF16),
        in_specs=[SMEM] + [VMEM] * 4,
        out_specs=VMEM,
        compiler_params=params(),
    )(core, xm, xt, w, bias)


def update_kernel(core, am, at, wm, wt, gm, out):
    rows, width = am.shape
    tile = pieces(rows)
    mine = pl.multiple_of(core[0] * width, width)
    other = pl.multiple_of(width - core[0] * width, width)

    for t in range(rows // tile):
        part = pl.ds(t * tile, tile)
        a = am[part, :]
        b = at[part, :]
        ym = two_dots(a, b, wm, mine, other, width)
        yt = two_dots(a, b, wt, mine, other, width)
        mean, scale = normalized(ym, yt)
        out[part, :] = ((ym - mean) * scale * gm[...]).astype(BF16)


def update_of(core, am, at, wm, wt, gm):
    return pl.pallas_call(
        update_kernel,
        out_shape=jax.ShapeDtypeStruct(am.shape, BF16),
        in_specs=[SMEM] + [VMEM] * 5,
        out_specs=VMEM,
        compiler_params=params(),
    )(core, am, at, wm, wt, gm)


def pick_rows_kernel(order_in, x_in, out, order, x, sems):
    copies = [
        pltpu.make_async_copy(order_in, order, sems.at[0]),
        pltpu.make_async_copy(x_in, x, sems.at[1]),
    ]
    for copy in copies:
        copy.start()
    for copy in copies:
        copy.wait()
    rows = x.shape[0]
    tile = pieces(rows)
    for t in range(rows // tile):
        part = pl.ds(t * tile, tile)
        ids = lax.broadcasted_iota(jnp.int32, (rows, tile), 0)
        chosen = jnp.where(ids == order[:, part], 1.0, 0.0).astype(BF16)
        out[part, :] = lax.dot_general(
            chosen, x[...], (((0,), (0,)), ((), ())), preferred_element_type=F32
        ).astype(BF16)


def pick_rows(order, x):
    return pl.pallas_call(
        pick_rows_kernel,
        out_shape=jax.ShapeDtypeStruct(x.shape, BF16),
        in_specs=[HBM] * 2,
        out_specs=VMEM,
        scratch_shapes=[
            pltpu.VMEM(order.shape, order.dtype),
            pltpu.VMEM(x.shape, x.dtype),
            pltpu.SemaphoreType.DMA((2,)),
        ],
        compiler_params=params(62),
    )(order, x)


def place_rows_kernel(order, x, rest, out):
    rows = x.shape[0]
    tile = pieces(rows)

    for t in range(rows // tile):
        start = t * tile
        part = pl.ds(start, tile)
        ids = lax.broadcasted_iota(jnp.int32, (tile, rows), 0) + start
        chosen = jnp.where(ids == order[...], 1.0, 0.0).astype(BF16)
        out[part, :] = (rest[part, :].astype(F32) + dot(chosen, x[...])).astype(BF16)


def place_rows(order, x, rest):
    return pl.pallas_call(
        place_rows_kernel,
        out_shape=jax.ShapeDtypeStruct(x.shape, BF16),
        in_specs=[VMEM] * 3,
        out_specs=VMEM,
        compiler_params=params(),
    )(order, x, rest)


def swap(x):
    return lax.ppermute(x, "feat", [(0, 1), (1, 0)])


def exchange(x):
    return lax.all_to_all(x, "nodes", split_axis=0, concat_axis=0, tiled=True)


def tie(*values):
    return lax.optimization_barrier(values)


def ring(chunk, pairs):
    return lax.ppermute(chunk, "nodes", pairs)


def local(
    grid_latent,
    mesh_latent,
    grid_order,
    enc_send_block,
    enc_recv_block,
    enc_offsets,
    enc_classes,
    enc_live,
    mesh_send_block,
    mesh_recv_block,
    mesh_offsets,
    mesh_classes,
    mesh_live,
    dec_send_block,
    dec_recv_block,
    dec_offsets,
    dec_classes,
    dec_live,
    class_gain,
    enc_weights,
    mesh_weights,
    dec_weights,
    enc_bias,
    enc_gain,
    mesh_bias,
    mesh_gain,
    dec_bias,
    dec_gain,
):
    rows, columns = mesh_latent.shape
    size = lax.axis_size("nodes")
    to_near = [(j, j ^ 1) for j in range(size)]
    onward = [(j, (j + 2 - 4 * (j % 2)) % size) for j in range(size)]
    core = lax.axis_index("feat").astype(jnp.int32).reshape(1)
    parity = (lax.axis_index("nodes") % 2).astype(jnp.int32).reshape(1)
    arrived = exchange(pick_rows(grid_order, grid_latent))

    chunks = math.gcd(CHUNKS, rows // BLOCK)
    prepared = prepare(
        rows // BLOCK,
        chunks,
        parity,
        class_gain,
        (enc_send_block, enc_recv_block, enc_live, enc_classes),
        (mesh_send_block, mesh_recv_block, mesh_live, mesh_classes),
        (dec_send_block, dec_recv_block, dec_live, dec_classes),
    )
    e_off = enc_offsets.reshape(-1, BLOCK)
    m_off = mesh_offsets.reshape(-1, BLOCK)
    d_off = dec_offsets.reshape(-1, BLOCK)
    outs = [enc_weights[2], mesh_weights[0, 2], mesh_weights[1, 2], dec_weights[2]]
    outs_other = [swap(outs[0])]
    gains = [enc_gain[None, :], mesh_gain]
    gains_other = [swap(x) for x in gains]
    xm, xt = mesh_latent, swap(mesh_latent)
    take = project(core, xm, xt, enc_weights[1], enc_bias[None, :])
    arrived, prepared, take, outs_other, gains_other = tie(
        arrived, prepared, take, outs_other, gains_other
    )
    gains = [gains[0], gains[1][:1], gains[1][1:]]
    gains_other = [gains_other[0], gains_other[1][:1], gains_other[1][1:]]
    e_list, m_list, d_list, counts, e_w, m_w, d_w = prepared
    length = list_length(mesh_send_block.shape[0])

    arrived_other = swap(arrived)
    nothing = jnp.zeros((1, columns), F32)
    send = project(core, arrived, arrived_other, enc_weights[0], nothing)
    agg = edge_sum(0, 0, counts, e_list, [send], take, e_off, e_w, None, True)
    grid_take = project(core, arrived, arrived_other, dec_weights[1], dec_bias[None, :])
    for r in range(ROUNDS):
        xm, xt, send = mix(
            core,
            agg,
            swap(agg),
            xm,
            xt,
            outs[r],
            outs_other[r],
            gains[r],
            gains_other[r],
            mesh_weights[r, 0],
        )
        near = [ring(x, to_near) for x in jnp.split(send, chunks)]
        take = project(core, xm, xt, mesh_weights[r, 1], mesh_bias[r][None, :])
        common = (take, m_off, m_w)
        total = edge_sum(2, 0, counts, m_list, [send], *common, None, False)
        fresh = outs[r + 1 : r + 2] if r + 1 < ROUNDS else outs[r + 1 :]
        fresh, total = tie(fresh, total)
        fresh = [swap(w) for w in fresh]
        far = []
        for k in range(chunks):
            near[k], total = tie(near[k], total)
            far.append(ring(near[k], onward))
        total = edge_sum(3, length, counts, m_list, near, *common, total, False)
        total, fresh = tie(total, fresh)
        outs_other += fresh
        if chunks > 1:
            total = edge_sum(
                4, 2 * length, counts, m_list, far[:-1], *common, total, False
            )
        agg = edge_sum(5, 3 * length, counts, m_list, far[-1:], *common, total, True)
    xm, xt, send = mix(
        core,
        agg,
        swap(agg),
        xm,
        xt,
        outs[ROUNDS],
        outs_other[ROUNDS],
        gains[ROUNDS],
        gains_other[ROUNDS],
        dec_weights[0],
    )
    agg = edge_sum(1, 0, counts, d_list, [send], grid_take, d_off, d_w, None, True)
    update = update_of(
        core, agg, swap(agg), outs[3], outs_other[3], dec_gain[None, :]
    )
    grid_out = place_rows(grid_order, exchange(update), grid_latent)
    return grid_out, xm


def solution(mesh):
    in_specs = (
        P("nodes", "feat"),
        P("nodes", "feat"),
        P("nodes", None),
        P("nodes"),
        P("nodes"),
        P("nodes", None, None),
        P("nodes", None),
        P("nodes"),
        P("nodes"),
        P("nodes"),
        P("nodes", None, None),
        P("nodes", None),
        P("nodes"),
        P("nodes"),
        P("nodes"),
        P("nodes", None, None),
        P("nodes", None),
        P("nodes"),
        P(),
        P(None, None, "feat"),
        P(None, None, None, "feat"),
        P(None, None, "feat"),
        P("feat"),
        P("feat"),
        P(None, "feat"),
        P(None, "feat"),
        P("feat"),
        P("feat"),
    )
    out_specs = (P("nodes", "feat"), P("nodes", "feat"))
    return jax.shard_map(local, mesh=mesh, in_specs=in_specs, out_specs=out_specs, check_vma=False)
```

```python
import functools
import math

import jax
import jax.numpy as jnp
from jax import lax
from jax.experimental import pallas as pl
from jax.experimental.pallas import tpu as pltpu
from jax.sharding import PartitionSpec as P


BLOCK = 128
ROUNDS = 2
UNROLL = 4
CHUNKS = 4
EPSILON = 1e-05

VMEM = pl.BlockSpec(memory_space=pltpu.VMEM)
SMEM = pl.BlockSpec(memory_space=pltpu.SMEM)
HBM = pl.BlockSpec(memory_space=pltpu.HBM)
F32 = jnp.float32
BF16 = jnp.bfloat16


def dot(a, b):
    return jnp.dot(a, b, preferred_element_type=F32)


def params(mib=24):
    return pltpu.CompilerParams(vmem_limit_bytes=mib << 20)


def pieces(rows):
    return min(rows, 256)


def entry(slot, sender, taker, total):
    return slot + sender * 256 + taker * 65536 + total * 16777216


def list_length(slots):
    return slots + 2 * UNROLL


def own_parts(chunks):
    return max(chunks - 1, 1)


def spread_weights(labels, gains, index):
    marks = labels[...]
    weight = jnp.zeros(marks.shape, F32)
    for k in range(gains.shape[1]):
        weight = jnp.where(marks == k, gains[index, k], weight)
    return weight


def prepare_kernel(blocks, chunks, parity, *refs):
    inputs, refs = refs[:13], refs[13:]
    (e_list, m_list, d_list, counts, e_w, m_w, d_w), refs = refs[:7], refs[7:]
    held, sems = refs[:13], refs[13]
    copies = [
        pltpu.make_async_copy(source, target, sems.at[k])
        for k, (source, target) in enumerate(zip(inputs, held))
    ]
    for copy in copies:
        copy.start()
    for copy in copies:
        copy.wait()
    gains, es, er, el, ec, ms, mr, ml, mc, ds, dr, dl, dc = held

    def finish(out, base, count):
        for k in range(2 * UNROLL):
            out[base + count + k] = entry(0, 0, 0, blocks)
        return jnp.maximum((count + UNROLL - 1) // UNROLL, 1)

    def plain(sends, takes, live, out, where):
        total = live[0]

        def step(i, carry):
            taker = takes[i]
            out[i] = entry(i, sends[i], taker, taker)
            return carry

        lax.fori_loop(0, total, step, 0)
        counts[where] = finish(out, 0, total)

    plain(es, er, el, e_list, 0)
    plain(ds, dr, dl, d_list, 1)
    length = list_length(ms.shape[0])
    first = jnp.where(parity[0] == 0, 2, 0)
    last = 2 - first
    per = blocks // chunks

    def step(i, carry):
        sender = ms[i]
        taker = mr[i]
        group = sender // blocks
        inner = sender - group * blocks
        late = inner >= blocks - per
        inner = jnp.where((group == last) & late, inner - (blocks - per), inner)
        turn = carry[-1]
        which = jnp.where(
            group == 1, 3 + turn, jnp.where(group == first, 0, jnp.where(late, 2, 1))
        )
        place = carry[0]
        for k in range(1, lists):
            place = jnp.where(which == k, length * k + carry[k], place)
        m_list[place] = entry(i, inner, taker, taker)
        turn = jnp.where(group == 1, turn + 1, turn)
        turn = jnp.where(turn == lists - 3, 0, turn)
        counted = [c + (which == k).astype(jnp.int32) for k, c in enumerate(carry[:-1])]
        return (*counted, turn)

    lists = 3 + own_parts(chunks)
    zero = tuple(jnp.int32(0) for _ in range(lists + 1))
    found = lax.fori_loop(0, ml[0], step, zero)
    for k, count in enumerate(found[:-1]):
        counts[2 + k] = finish(m_list, length * k, count)

    for index, (labels, out) in enumerate(((ec, e_w), (mc, m_w), (dc, d_w))):
        out[...] = spread_weights(labels, gains, index)


def prepare(blocks, chunks, parity, gains, enc, mesh, dec):
    i32 = jnp.int32
    sets = (enc, mesh, dec)
    slots = [s[0].shape[0] for s in sets]
    sizes = [list_length(slots[0]), (3 + own_parts(chunks)) * list_length(slots[1])]
    sizes += [list_length(slots[2]), 8 + chunks]
    out_shape = [jax.ShapeDtypeStruct((n,), i32) for n in sizes]
    out_shape += [jax.ShapeDtypeStruct((n, BLOCK), F32) for n in slots]
    arrays = [gains, *enc, *mesh, *dec]
    spaces = [pltpu.SMEM] + [pltpu.SMEM, pltpu.SMEM, pltpu.SMEM, pltpu.VMEM] * 3
    scratch = [space(x.shape, x.dtype) for space, x in zip(spaces, arrays)]
    scratch.append(pltpu.SemaphoreType.DMA((len(arrays),)))
    return pl.pallas_call(
        functools.partial(prepare_kernel, blocks, chunks),
        out_shape=out_shape,
        in_specs=[SMEM] + [HBM] * len(arrays),
        out_specs=[SMEM] * 4 + [VMEM] * 3,
        scratch_shapes=scratch,
        compiler_params=params(4),
        cost_estimate=pl.CostEstimate(
            flops=2_000_000_000, bytes_accessed=1_000_000, transcendentals=0
        ),
    )(parity, *arrays)


def edge_loop(base, trips, items, send, take, offsets, weights, acc, picks, held):
    rows = lax.broadcasted_iota(jnp.int32, (BLOCK, BLOCK), 0).astype(F32).astype(BF16)
    one = jnp.ones((BLOCK, BLOCK), BF16)
    nil = jnp.zeros((BLOCK, BLOCK), BF16)

    def spread(row):
        return jnp.broadcast_to(row.astype(F32).astype(BF16), (BLOCK, BLOCK))

    def build(i):
        for u in range(UNROLL):
            slot = items[base + i * UNROLL + u] & 255
            both = [
                jnp.where(rows == spread(offsets[pl.ds(2 * slot + k, 1), :]), one, nil)
                for k in range(2)
            ]
            picks[u] = jnp.concatenate([x.T for x in both], axis=1)

    def gather(i):
        for u in range(UNROLL):
            item = items[base + i * UNROLL + u]
            sender = pl.multiple_of(((item >> 8) & 255) * BLOCK, BLOCK)
            taker = pl.multiple_of(((item >> 16) & 255) * BLOCK, BLOCK)
            both = jnp.concatenate(
                [send[pl.ds(sender, BLOCK), :], take[pl.ds(taker, BLOCK), :]], axis=0
            )
            half = dot(picks[u], both)
            held[u] = (half + half * jnp.tanh(half)).astype(BF16)

    def scatter(i):
        for u in range(UNROLL):
            item = items[base + i * UNROLL + u]
            slot = item & 255
            total = pl.multiple_of((item >> 24) * BLOCK, BLOCK)
            is_to = rows == spread(offsets[pl.ds(2 * slot + 1, 1), :])
            put = jnp.where(is_to, spread(weights[pl.ds(slot, 1), :]), nil)
            acc[pl.ds(total, BLOCK), :] += dot(put, held[u])

    def turn(i, carry):
        scatter(i - 1)
        gather(i)
        build(i + 1)
        return carry

    build(0)
    gather(0)
    build(1)
    lax.fori_loop(1, trips, turn, 0)
    scatter(trips - 1)


def edge_kernel(where, base, pieces_in, first, last, counts, items, *refs):
    refs = list(refs)
    sends = [refs.pop(0) for _ in range(pieces_in)]
    take, offsets, weights = refs[:3]
    refs = refs[3:]
    if not first:
        before = refs.pop(0)
    out, picks, held = refs[:3]
    refs = refs[3:]
    acc = refs.pop(0) if last else out
    if first:
        acc[...] = jnp.zeros_like(acc)
    elif last:
        acc[...] = before[...]
    send = sends[0]
    if pieces_in > 1:
        joined = refs.pop(0)
        depth = send.shape[0]
        for k, piece in enumerate(sends):
            joined[pl.ds(k * depth, depth), :] = piece[...]
        send = joined
    edge_loop(base, counts[where], items, send, take, offsets, weights, acc, picks, held)
    if last:
        out[...] = acc[pl.ds(0, out.shape[0]), :].astype(out.dtype)


def edge_sum(where, base, counts, items, sends, take, offsets, weights, before, last):
    first = before is None
    rows, columns = take.shape
    arrays = [counts, items, *sends, take, offsets, weights]
    aliases = {}
    if not first:
        if not last:
            aliases = {len(arrays): 0}
        arrays.append(before)
    full = (rows + BLOCK, columns)
    scratch = [
        pltpu.VMEM((UNROLL, BLOCK, width), BF16) for width in (2 * BLOCK, columns)
    ]
    if last:
        scratch.append(pltpu.VMEM(full, F32))
        shape = jax.ShapeDtypeStruct((rows, columns), BF16)
    else:
        shape = jax.ShapeDtypeStruct(full, F32)
    if len(sends) > 1:
        depth = sum(x.shape[0] for x in sends)
        scratch.append(pltpu.VMEM((depth, columns), BF16))
    return pl.pallas_call(
        functools.partial(edge_kernel, where, base, len(sends), first, last),
        out_shape=shape,
        in_specs=[SMEM, SMEM] + [VMEM] * (len(arrays) - 2),
        out_specs=VMEM,
        scratch_shapes=scratch,
        input_output_aliases=aliases,
        compiler_params=params(),
        cost_estimate=pl.CostEstimate(
            flops=2_000_000_000, bytes_accessed=2_000_000, transcendentals=1_000_000
        ),
    )(*arrays)


def two_dots(a, b, weights, mine, other, width):
    return dot(a, weights[pl.ds(mine, width), :]) + dot(b, weights[pl.ds(other, width), :])


def normalized(ym, yt):
    width = ym.shape[1] + yt.shape[1]
    total = jnp.sum(ym + yt, axis=1, keepdims=True)
    squares = jnp.sum(ym * ym + yt * yt, axis=1, keepdims=True)
    mean = total / width
    spread = squares / width - mean * mean
    return mean, lax.rsqrt(spread + EPSILON)


def mix_kernel(
    core, am, at, xm, xt, wm, wt, gm, gt, ws, out_m, out_t, out_s
):
    rows, width = am.shape
    tile = pieces(rows)
    mine = pl.multiple_of(core[0] * width, width)
    other = pl.multiple_of(width - core[0] * width, width)

    for t in range(rows // tile):
        part = pl.ds(t * tile, tile)
        a = am[part, :]
        b = at[part, :]
        ym = two_dots(a, b, wm, mine, other, width)
        yt = two_dots(a, b, wt, mine, other, width)
        mean, scale = normalized(ym, yt)
        nm = (xm[part, :].astype(F32) + (ym - mean) * scale * gm[...]).astype(BF16)
        nt = (xt[part, :].astype(F32) + (yt - mean) * scale * gt[...]).astype(BF16)
        out_m[part, :] = nm
        out_t[part, :] = nt
        out_s[part, :] = (0.5 * two_dots(nm, nt, ws, mine, other, width)).astype(BF16)


def mix(core, am, at, xm, xt, wm, wt, gm, gt, ws):
    shape = jax.ShapeDtypeStruct(am.shape, BF16)
    return pl.pallas_call(
        mix_kernel,
        out_shape=[shape] * 3,
        in_specs=[SMEM] + [VMEM] * 9,
        out_specs=[VMEM] * 3,
        compiler_params=params(),
    )(core, am, at, xm, xt, wm, wt, gm, gt, ws)


def project_kernel(core, xm, xt, w, bias, out):
    rows, width = xm.shape
    tile = pieces(rows)
    mine = pl.multiple_of(core[0] * width, width)
    other = pl.multiple_of(width - core[0] * width, width)

    for t in range(rows // tile):
        part = pl.ds(t * tile, tile)
        y = two_dots(xm[part, :], xt[part, :], w, mine, other, width)
        out[part, :] = (0.5 * (y + bias[...])).astype(BF16)


def project(core, xm, xt, w, bias):
    return pl.pallas_call(
        project_kernel,
        out_shape=jax.ShapeDtypeStruct(xm.shape, BF16),
        in_specs=[SMEM] + [VMEM] * 4,
        out_specs=VMEM,
        compiler_params=params(),
    )(core, xm, xt, w, bias)


def update_kernel(core, am, at, wm, wt, gm, out):
    rows, width = am.shape
    tile = pieces(rows)
    mine = pl.multiple_of(core[0] * width, width)
    other = pl.multiple_of(width - core[0] * width, width)

    for t in range(rows // tile):
        part = pl.ds(t * tile, tile)
        a = am[part, :]
        b = at[part, :]
        ym = two_dots(a, b, wm, mine, other, width)
        yt = two_dots(a, b, wt, mine, other, width)
        mean, scale = normalized(ym, yt)
        out[part, :] = ((ym - mean) * scale * gm[...]).astype(BF16)


def update_of(core, am, at, wm, wt, gm):
    return pl.pallas_call(
        update_kernel,
        out_shape=jax.ShapeDtypeStruct(am.shape, BF16),
        in_specs=[SMEM] + [VMEM] * 5,
        out_specs=VMEM,
        compiler_params=params(),
    )(core, am, at, wm, wt, gm)


def pick_rows_kernel(order_in, x_in, out, order, x, sems):
    copies = [
        pltpu.make_async_copy(order_in, order, sems.at[0]),
        pltpu.make_async_copy(x_in, x, sems.at[1]),
    ]
    for copy in copies:
        copy.start()
    for copy in copies:
        copy.wait()
    rows = x.shape[0]
    tile = pieces(rows)
    for t in range(rows // tile):
        part = pl.ds(t * tile, tile)
        ids = lax.broadcasted_iota(jnp.int32, (rows, tile), 0)
        chosen = jnp.where(ids == order[:, part], 1.0, 0.0).astype(BF16)
        out[part, :] = lax.dot_general(
            chosen, x[...], (((0,), (0,)), ((), ())), preferred_element_type=F32
        ).astype(BF16)


def pick_rows(order, x):
    return pl.pallas_call(
        pick_rows_kernel,
        out_shape=jax.ShapeDtypeStruct(x.shape, BF16),
        in_specs=[HBM] * 2,
        out_specs=VMEM,
        scratch_shapes=[
            pltpu.VMEM(order.shape, order.dtype),
            pltpu.VMEM(x.shape, x.dtype),
            pltpu.SemaphoreType.DMA((2,)),
        ],
        compiler_params=params(62),
    )(order, x)


def place_rows_kernel(order, x, rest, out):
    rows = x.shape[0]
    tile = pieces(rows)

    for t in range(rows // tile):
        start = t * tile
        part = pl.ds(start, tile)
        ids = lax.broadcasted_iota(jnp.int32, (tile, rows), 0) + start
        chosen = jnp.where(ids == order[...], 1.0, 0.0).astype(BF16)
        out[part, :] = (rest[part, :].astype(F32) + dot(chosen, x[...])).astype(BF16)


def place_rows(order, x, rest):
    return pl.pallas_call(
        place_rows_kernel,
        out_shape=jax.ShapeDtypeStruct(x.shape, BF16),
        in_specs=[VMEM] * 3,
        out_specs=VMEM,
        compiler_params=params(),
    )(order, x, rest)


def swap(x):
    return lax.ppermute(x, "feat", [(0, 1), (1, 0)])


def exchange(x):
    return lax.all_to_all(x, "nodes", split_axis=0, concat_axis=0, tiled=True)


def tie(*values):
    return lax.optimization_barrier(values)


def ring(chunk, pairs):
    return lax.ppermute(chunk, "nodes", pairs)


def local(
    grid_latent,
    mesh_latent,
    grid_order,
    enc_send_block,
    enc_recv_block,
    enc_offsets,
    enc_classes,
    enc_live,
    mesh_send_block,
    mesh_recv_block,
    mesh_offsets,
    mesh_classes,
    mesh_live,
    dec_send_block,
    dec_recv_block,
    dec_offsets,
    dec_classes,
    dec_live,
    class_gain,
    enc_weights,
    mesh_weights,
    dec_weights,
    enc_bias,
    enc_gain,
    mesh_bias,
    mesh_gain,
    dec_bias,
    dec_gain,
):
    rows, columns = mesh_latent.shape
    size = lax.axis_size("nodes")
    to_near = [(j, j ^ 1) for j in range(size)]
    onward = [(j, (j + 2 - 4 * (j % 2)) % size) for j in range(size)]
    core = lax.axis_index("feat").astype(jnp.int32).reshape(1)
    parity = (lax.axis_index("nodes") % 2).astype(jnp.int32).reshape(1)
    arrived = exchange(pick_rows(grid_order, grid_latent))

    chunks = math.gcd(CHUNKS, rows // BLOCK)
    prepared = prepare(
        rows // BLOCK,
        chunks,
        parity,
        class_gain,
        (enc_send_block, enc_recv_block, enc_live, enc_classes),
        (mesh_send_block, mesh_recv_block, mesh_live, mesh_classes),
        (dec_send_block, dec_recv_block, dec_live, dec_classes),
    )
    e_off = enc_offsets.reshape(-1, BLOCK)
    m_off = mesh_offsets.reshape(-1, BLOCK)
    d_off = dec_offsets.reshape(-1, BLOCK)
    outs = [enc_weights[2], mesh_weights[0, 2], mesh_weights[1, 2], dec_weights[2]]
    outs_other = [swap(outs[0])]
    gains = [enc_gain[None, :], mesh_gain]
    gains_other = [swap(x) for x in gains]
    xm, xt = mesh_latent, swap(mesh_latent)
    take = project(core, xm, xt, enc_weights[1], enc_bias[None, :])
    arrived, prepared, take, outs_other, gains_other = tie(
        arrived, prepared, take, outs_other, gains_other
    )
    gains = [gains[0], gains[1][:1], gains[1][1:]]
    gains_other = [gains_other[0], gains_other[1][:1], gains_other[1][1:]]
    e_list, m_list, d_list, counts, e_w, m_w, d_w = prepared
    length = list_length(mesh_send_block.shape[0])

    arrived_other = swap(arrived)
    nothing = jnp.zeros((1, columns), F32)
    send = project(core, arrived, arrived_other, enc_weights[0], nothing)
    agg = edge_sum(0, 0, counts, e_list, [send], take, e_off, e_w, None, True)
    grid_take = project(core, arrived, arrived_other, dec_weights[1], dec_bias[None, :])
    for r in range(ROUNDS):
        xm, xt, send = mix(
            core,
            agg,
            swap(agg),
            xm,
            xt,
            outs[r],
            outs_other[r],
            gains[r],
            gains_other[r],
            mesh_weights[r, 0],
        )
        near = [ring(x, to_near) for x in jnp.split(send, chunks)]
        take = project(core, xm, xt, mesh_weights[r, 1], mesh_bias[r][None, :])
        common = (take, m_off, m_w)
        total = None
        far = []
        for k in range(chunks):
            if total is None:
                near[k], take = tie(near[k], take)
                common = (take, m_off, m_w)
            else:
                near[k], total = tie(near[k], total)
            far.append(ring(near[k], onward))
            if k < own_parts(chunks):
                total = edge_sum(
                    5 + k,
                    (3 + k) * length,
                    counts,
                    m_list,
                    [send],
                    *common,
                    total,
                    False,
                )
        fresh = outs[r + 1 : r + 2] if r + 1 < ROUNDS else outs[r + 1 :]
        fresh, total = tie(fresh, total)
        fresh = [swap(w) for w in fresh]
        total = edge_sum(2, 0, counts, m_list, near, *common, total, False)
        total, fresh = tie(total, fresh)
        outs_other += fresh
        if chunks > 1:
            total = edge_sum(3, length, counts, m_list, far[:-1], *common, total, False)
        agg = edge_sum(4, 2 * length, counts, m_list, far[-1:], *common, total, True)
    xm, xt, send = mix(
        core,
        agg,
        swap(agg),
        xm,
        xt,
        outs[ROUNDS],
        outs_other[ROUNDS],
        gains[ROUNDS],
        gains_other[ROUNDS],
        dec_weights[0],
    )
    agg = edge_sum(1, 0, counts, d_list, [send], grid_take, d_off, d_w, None, True)
    update = update_of(
        core, agg, swap(agg), outs[3], outs_other[3], dec_gain[None, :]
    )
    grid_out = place_rows(grid_order, exchange(update), grid_latent)
    return grid_out, xm


def solution(mesh):
    in_specs = (
        P("nodes", "feat"),
        P("nodes", "feat"),
        P("nodes", None),
        P("nodes"),
        P("nodes"),
        P("nodes", None, None),
        P("nodes", None),
        P("nodes"),
        P("nodes"),
        P("nodes"),
        P("nodes", None, None),
        P("nodes", None),
        P("nodes"),
        P("nodes"),
        P("nodes"),
        P("nodes", None, None),
        P("nodes", None),
        P("nodes"),
        P(),
        P(None, None, "feat"),
        P(None, None, None, "feat"),
        P(None, None, "feat"),
        P("feat"),
        P("feat"),
        P(None, "feat"),
        P(None, "feat"),
        P("feat"),
        P("feat"),
    )
    out_specs = (P("nodes", "feat"), P("nodes", "feat"))
    return jax.shard_map(
        local, mesh=mesh, in_specs=in_specs, out_specs=out_specs, check_vma=False
    )
```

```python
import functools
import math

import jax
import jax.numpy as jnp
from jax import lax
from jax.experimental import pallas as pl
from jax.experimental.pallas import tpu as pltpu
from jax.sharding import PartitionSpec as P


BLOCK = 128
ROUNDS = 2
UNROLL = 4
CHUNKS = 4
HALVES = 2
EPSILON = 1e-05

VMEM = pl.BlockSpec(memory_space=pltpu.VMEM)
SMEM = pl.BlockSpec(memory_space=pltpu.SMEM)
HBM = pl.BlockSpec(memory_space=pltpu.HBM)
F32 = jnp.float32
BF16 = jnp.bfloat16


def dot(a, b):
    return jnp.dot(a, b, preferred_element_type=F32)


def params(mib=24):
    return pltpu.CompilerParams(vmem_limit_bytes=mib << 20)


def pieces(rows):
    return min(rows, 256)


def entry(slot, sender, taker, total):
    return slot + sender * 256 + taker * 65536 + total * 16777216


def list_length(slots):
    return slots + 2 * UNROLL


def own_parts(chunks):
    return max(chunks - 1, 1)


def spread_weights(labels, gains, index):
    marks = labels[...]
    weight = jnp.zeros(marks.shape, F32)
    for k in range(gains.shape[1]):
        weight = jnp.where(marks == k, gains[index, k], weight)
    return weight


def prepare_kernel(blocks, chunks, parity, *refs):
    inputs, refs = refs[:13], refs[13:]
    (e_list, m_list, d_list, counts, e_w, m_w, d_w), refs = refs[:7], refs[7:]
    held, sems = refs[:13], refs[13]
    copies = [
        pltpu.make_async_copy(source, target, sems.at[k])
        for k, (source, target) in enumerate(zip(inputs, held))
    ]
    for copy in copies:
        copy.start()
    for copy in copies:
        copy.wait()
    gains, es, er, el, ec, ms, mr, ml, mc, ds, dr, dl, dc = held

    def finish(out, base, count):
        for k in range(2 * UNROLL):
            out[base + count + k] = entry(0, 0, 0, blocks)
        return jnp.maximum((count + UNROLL - 1) // UNROLL, 1)

    def plain(sends, takes, live, out, where):
        total = live[0]

        def step(i, carry):
            taker = takes[i]
            out[i] = entry(i, sends[i], taker, taker)
            return carry

        lax.fori_loop(0, total, step, 0)
        counts[where] = finish(out, 0, total)

    plain(es, er, el, e_list, 0)
    plain(ds, dr, dl, d_list, 1)
    length = list_length(ms.shape[0])
    first = jnp.where(parity[0] == 0, 2, 0)
    last = 2 - first
    per = blocks // chunks

    def step(i, carry):
        sender = ms[i]
        taker = mr[i]
        group = sender // blocks
        inner = sender - group * blocks
        late = inner >= blocks - per
        inner = jnp.where((group == last) & late, inner - (blocks - per), inner)
        turn = carry[-1]
        which = jnp.where(
            group == 1, 3 + turn, jnp.where(group == first, 0, jnp.where(late, 2, 1))
        )
        place = carry[0]
        for k in range(1, lists):
            place = jnp.where(which == k, length * k + carry[k], place)
        m_list[place] = entry(i, inner, taker, taker)
        turn = jnp.where(group == 1, turn + 1, turn)
        turn = jnp.where(turn == lists - 3, 0, turn)
        counted = [c + (which == k).astype(jnp.int32) for k, c in enumerate(carry[:-1])]
        return (*counted, turn)

    lists = 3 + own_parts(chunks)
    zero = tuple(jnp.int32(0) for _ in range(lists + 1))
    found = lax.fori_loop(0, ml[0], step, zero)
    for k, count in enumerate(found[:-1]):
        counts[2 + k] = finish(m_list, length * k, count)

    for index, (labels, out) in enumerate(((ec, e_w), (mc, m_w), (dc, d_w))):
        out[...] = spread_weights(labels, gains, index)


def prepare(blocks, chunks, parity, gains, enc, mesh, dec):
    i32 = jnp.int32
    sets = (enc, mesh, dec)
    slots = [s[0].shape[0] for s in sets]
    sizes = [list_length(slots[0]), (3 + own_parts(chunks)) * list_length(slots[1])]
    sizes += [list_length(slots[2]), 8 + chunks]
    out_shape = [jax.ShapeDtypeStruct((n,), i32) for n in sizes]
    out_shape += [jax.ShapeDtypeStruct((n, BLOCK), F32) for n in slots]
    arrays = [gains, *enc, *mesh, *dec]
    spaces = [pltpu.SMEM] + [pltpu.SMEM, pltpu.SMEM, pltpu.SMEM, pltpu.VMEM] * 3
    scratch = [space(x.shape, x.dtype) for space, x in zip(spaces, arrays)]
    scratch.append(pltpu.SemaphoreType.DMA((len(arrays),)))
    return pl.pallas_call(
        functools.partial(prepare_kernel, blocks, chunks),
        out_shape=out_shape,
        in_specs=[SMEM] + [HBM] * len(arrays),
        out_specs=[SMEM] * 4 + [VMEM] * 3,
        scratch_shapes=scratch,
        compiler_params=params(4),
        cost_estimate=pl.CostEstimate(
            flops=2_000_000_000, bytes_accessed=1_000_000, transcendentals=0
        ),
    )(parity, *arrays)


def edge_loop(base, trips, items, send, take, offsets, weights, acc, picks, held):
    rows = lax.broadcasted_iota(jnp.int32, (BLOCK, BLOCK), 0).astype(F32).astype(BF16)
    one = jnp.ones((BLOCK, BLOCK), BF16)
    nil = jnp.zeros((BLOCK, BLOCK), BF16)

    def spread(row):
        return jnp.broadcast_to(row.astype(F32).astype(BF16), (BLOCK, BLOCK))

    def build(i):
        for u in range(UNROLL):
            slot = items[base + i * UNROLL + u] & 255
            both = [
                jnp.where(rows == spread(offsets[pl.ds(2 * slot + k, 1), :]), one, nil)
                for k in range(2)
            ]
            picks[u] = jnp.concatenate([x.T for x in both], axis=1)

    def gather(i):
        for u in range(UNROLL):
            item = items[base + i * UNROLL + u]
            sender = pl.multiple_of(((item >> 8) & 255) * BLOCK, BLOCK)
            taker = pl.multiple_of(((item >> 16) & 255) * BLOCK, BLOCK)
            both = jnp.concatenate(
                [send[pl.ds(sender, BLOCK), :], take[pl.ds(taker, BLOCK), :]], axis=0
            )
            half = dot(picks[u], both)
            held[u] = (half + half * jnp.tanh(half)).astype(BF16)

    def scatter(i):
        for u in range(UNROLL):
            item = items[base + i * UNROLL + u]
            slot = item & 255
            total = pl.multiple_of((item >> 24) * BLOCK, BLOCK)
            is_to = rows == spread(offsets[pl.ds(2 * slot + 1, 1), :])
            put = jnp.where(is_to, spread(weights[pl.ds(slot, 1), :]), nil)
            acc[pl.ds(total, BLOCK), :] += dot(put, held[u])

    def turn(i, carry):
        scatter(i - 1)
        gather(i)
        build(i + 1)
        return carry

    build(0)
    gather(0)
    build(1)
    lax.fori_loop(1, trips, turn, 0)
    scatter(trips - 1)


def edge_kernel(where, base, pieces_in, halves, first, counts, items, *refs):
    last = halves > 0
    refs = list(refs)
    sends = [refs.pop(0) for _ in range(pieces_in)]
    take, offsets, weights = refs[:3]
    refs = refs[3:]
    if not first:
        before = refs.pop(0)
    outs = refs[: max(halves, 1)]
    refs = refs[max(halves, 1) :]
    picks, held = refs[:2]
    refs = refs[2:]
    acc = refs.pop(0) if last else outs[0]
    if first:
        acc[...] = jnp.zeros_like(acc)
    elif last:
        acc[...] = before[...]
    send = sends[0]
    if pieces_in > 1:
        joined = refs.pop(0)
        depth = send.shape[0]
        for k, piece in enumerate(sends):
            joined[pl.ds(k * depth, depth), :] = piece[...]
        send = joined
    edge_loop(base, counts[where], items, send, take, offsets, weights, acc, picks, held)
    for k, out in enumerate(outs[:halves]):
        depth = out.shape[0]
        out[...] = acc[pl.ds(k * depth, depth), :].astype(out.dtype)


def edge_sum(where, base, counts, items, sends, take, offsets, weights, before, halves):
    last = halves > 0
    first = before is None
    rows, columns = take.shape
    arrays = [counts, items, *sends, take, offsets, weights]
    aliases = {}
    if not first:
        if not last:
            aliases = {len(arrays): 0}
        arrays.append(before)
    full = (rows + BLOCK, columns)
    scratch = [
        pltpu.VMEM((UNROLL, BLOCK, width), BF16) for width in (2 * BLOCK, columns)
    ]
    if last:
        scratch.append(pltpu.VMEM(full, F32))
        shape = [jax.ShapeDtypeStruct((rows // halves, columns), BF16)] * halves
    else:
        shape = [jax.ShapeDtypeStruct(full, F32)]
    if len(sends) > 1:
        depth = sum(x.shape[0] for x in sends)
        scratch.append(pltpu.VMEM((depth, columns), BF16))
    result = pl.pallas_call(
        functools.partial(edge_kernel, where, base, len(sends), halves, first),
        out_shape=shape,
        in_specs=[SMEM, SMEM] + [VMEM] * (len(arrays) - 2),
        out_specs=[VMEM] * len(shape),
        scratch_shapes=scratch,
        input_output_aliases=aliases,
        compiler_params=params(),
        cost_estimate=pl.CostEstimate(
            flops=2_000_000_000, bytes_accessed=2_000_000, transcendentals=1_000_000
        ),
    )(*arrays)
    return list(result) if last else result[0]


def two_dots(a, b, weights, mine, other, width):
    return dot(a, weights[pl.ds(mine, width), :]) + dot(b, weights[pl.ds(other, width), :])


def normalized(ym, yt):
    width = ym.shape[1] + yt.shape[1]
    total = jnp.sum(ym + yt, axis=1, keepdims=True)
    squares = jnp.sum(ym * ym + yt * yt, axis=1, keepdims=True)
    mean = total / width
    spread = squares / width - mean * mean
    return mean, lax.rsqrt(spread + EPSILON)


def mix_kernel(
    chunks, core, am, at, xm, xt, wm, wt, gm, gt, ws, out_m, *outs
):
    rows, width = am.shape
    out_s, out_t = outs[:chunks], outs[chunks:]
    tile = rows // chunks
    mine = pl.multiple_of(core[0] * width, width)
    other = pl.multiple_of(width - core[0] * width, width)

    for t in range(rows // tile):
        part = pl.ds(t * tile, tile)
        a = am[part, :]
        b = at[part, :]
        ym = two_dots(a, b, wm, mine, other, width)
        yt = two_dots(a, b, wt, mine, other, width)
        mean, scale = normalized(ym, yt)
        nm = (xm[part, :].astype(F32) + (ym - mean) * scale * gm[...]).astype(BF16)
        nt = (xt[part, :].astype(F32) + (yt - mean) * scale * gt[...]).astype(BF16)
        out_m[part, :] = nm
        for out in out_t:
            out[part, :] = nt
        out_s[t][...] = (0.5 * two_dots(nm, nt, ws, mine, other, width)).astype(BF16)


def mix(chunks, last, core, am, at, xm, xt, wm, wt, gm, gt, ws):
    rows, width = am.shape
    shapes = [jax.ShapeDtypeStruct((rows, width), BF16)]
    shapes += [jax.ShapeDtypeStruct((rows // chunks, width), BF16)] * chunks
    shapes += shapes[:1] * (not last)
    new_xm, *rest = pl.pallas_call(
        functools.partial(mix_kernel, chunks),
        out_shape=shapes,
        in_specs=[SMEM] + [VMEM] * 9,
        out_specs=[VMEM] * len(shapes),
        compiler_params=params(),
    )(core, am, at, xm, xt, wm, wt, gm, gt, ws)
    return new_xm, rest[:chunks], rest[chunks:]


def mix_halves(chunks, last, core, aggs, xms, xts, *rest):
    others = [swap(x) for x in aggs]
    results = [
        mix(chunks // len(aggs), last, core, am, at, xm, xt, *rest)
        for am, at, xm, xt in zip(aggs, others, xms, xts)
    ]
    send = [x for _, part, _ in results for x in part]
    return [x for x, _, _ in results], [x for _, _, t in results for x in t], send


def copy_kernel(*refs):
    ins, out = refs[:-1], refs[-1]
    depth = ins[0].shape[0]
    for k, x in enumerate(ins):
        out[pl.ds(k * depth, depth), :] = x[...]


def joined_rows(xs):
    rows, width = xs[0].shape
    return pl.pallas_call(
        copy_kernel,
        out_shape=jax.ShapeDtypeStruct((rows * len(xs), width), BF16),
        in_specs=[VMEM] * len(xs),
        out_specs=VMEM,
        compiler_params=params(4),
    )(*xs)


def project_kernel(core, *refs):
    w, bias, out = refs[-3:]
    parts = len(refs[:-3]) // 2
    depth, width = refs[0].shape
    rows = depth * parts
    tile = pieces(depth)
    mine = pl.multiple_of(core[0] * width, width)
    other = pl.multiple_of(width - core[0] * width, width)

    for t in range(rows // tile):
        part = pl.ds(t * tile, tile)
        which, inner = divmod(t * tile, depth)
        inner = pl.ds(inner, tile)
        xm, xt = refs[which], refs[parts + which]
        y = two_dots(xm[inner, :], xt[inner, :], w, mine, other, width)
        out[part, :] = (0.5 * (y + bias[...])).astype(BF16)


def project(core, xm, xt, w, bias):
    rows, width = xm[0].shape
    return pl.pallas_call(
        project_kernel,
        out_shape=jax.ShapeDtypeStruct((rows * len(xm), width), BF16),
        in_specs=[SMEM] + [VMEM] * (2 * len(xm) + 2),
        out_specs=VMEM,
        compiler_params=params(),
    )(core, *xm, *xt, w, bias)


def update_kernel(core, am, at, wm, wt, gm, out):
    rows, width = am.shape
    tile = pieces(rows)
    mine = pl.multiple_of(core[0] * width, width)
    other = pl.multiple_of(width - core[0] * width, width)

    for t in range(rows // tile):
        part = pl.ds(t * tile, tile)
        a = am[part, :]
        b = at[part, :]
        ym = two_dots(a, b, wm, mine, other, width)
        yt = two_dots(a, b, wt, mine, other, width)
        mean, scale = normalized(ym, yt)
        out[part, :] = ((ym - mean) * scale * gm[...]).astype(BF16)


def update_of(core, am, at, wm, wt, gm):
    return pl.pallas_call(
        update_kernel,
        out_shape=jax.ShapeDtypeStruct(am.shape, BF16),
        in_specs=[SMEM] + [VMEM] * 5,
        out_specs=VMEM,
        compiler_params=params(),
    )(core, am, at, wm, wt, gm)


def pick_rows_kernel(order_in, x_in, out, order, x, sems):
    copies = [
        pltpu.make_async_copy(order_in, order, sems.at[0]),
        pltpu.make_async_copy(x_in, x, sems.at[1]),
    ]
    for copy in copies:
        copy.start()
    for copy in copies:
        copy.wait()
    rows = x.shape[0]
    tile = pieces(rows)
    for t in range(rows // tile):
        part = pl.ds(t * tile, tile)
        ids = lax.broadcasted_iota(jnp.int32, (rows, tile), 0)
        chosen = jnp.where(ids == order[:, part], 1.0, 0.0).astype(BF16)
        out[part, :] = lax.dot_general(
            chosen, x[...], (((0,), (0,)), ((), ())), preferred_element_type=F32
        ).astype(BF16)


def pick_rows(order, x):
    return pl.pallas_call(
        pick_rows_kernel,
        out_shape=jax.ShapeDtypeStruct(x.shape, BF16),
        in_specs=[HBM] * 2,
        out_specs=VMEM,
        scratch_shapes=[
            pltpu.VMEM(order.shape, order.dtype),
            pltpu.VMEM(x.shape, x.dtype),
            pltpu.SemaphoreType.DMA((2,)),
        ],
        compiler_params=params(62),
    )(order, x)


def place_rows_kernel(order, x, rest, out):
    rows = x.shape[0]
    tile = pieces(rows)

    for t in range(rows // tile):
        start = t * tile
        part = pl.ds(start, tile)
        ids = lax.broadcasted_iota(jnp.int32, (tile, rows), 0) + start
        chosen = jnp.where(ids == order[...], 1.0, 0.0).astype(BF16)
        out[part, :] = (rest[part, :].astype(F32) + dot(chosen, x[...])).astype(BF16)


def place_rows(order, x, rest):
    return pl.pallas_call(
        place_rows_kernel,
        out_shape=jax.ShapeDtypeStruct(x.shape, BF16),
        in_specs=[VMEM] * 3,
        out_specs=VMEM,
        compiler_params=params(),
    )(order, x, rest)


def swap(x):
    return lax.ppermute(x, "feat", [(0, 1), (1, 0)])


def exchange(x):
    return lax.all_to_all(x, "nodes", split_axis=0, concat_axis=0, tiled=True)


def tie(*values):
    return lax.optimization_barrier(values)


def ring(chunk, pairs):
    return lax.ppermute(chunk, "nodes", pairs)


def local(
    grid_latent,
    mesh_latent,
    grid_order,
    enc_send_block,
    enc_recv_block,
    enc_offsets,
    enc_classes,
    enc_live,
    mesh_send_block,
    mesh_recv_block,
    mesh_offsets,
    mesh_classes,
    mesh_live,
    dec_send_block,
    dec_recv_block,
    dec_offsets,
    dec_classes,
    dec_live,
    class_gain,
    enc_weights,
    mesh_weights,
    dec_weights,
    enc_bias,
    enc_gain,
    mesh_bias,
    mesh_gain,
    dec_bias,
    dec_gain,
):
    rows, columns = mesh_latent.shape
    size = lax.axis_size("nodes")
    to_near = [(j, j ^ 1) for j in range(size)]
    onward = [(j, (j + 2 - 4 * (j % 2)) % size) for j in range(size)]
    core = lax.axis_index("feat").astype(jnp.int32).reshape(1)
    parity = (lax.axis_index("nodes") % 2).astype(jnp.int32).reshape(1)
    arrived = exchange(pick_rows(grid_order, grid_latent))

    chunks = math.gcd(CHUNKS, rows // BLOCK)
    prepared = prepare(
        rows // BLOCK,
        chunks,
        parity,
        class_gain,
        (enc_send_block, enc_recv_block, enc_live, enc_classes),
        (mesh_send_block, mesh_recv_block, mesh_live, mesh_classes),
        (dec_send_block, dec_recv_block, dec_live, dec_classes),
    )
    e_off = enc_offsets.reshape(-1, BLOCK)
    m_off = mesh_offsets.reshape(-1, BLOCK)
    d_off = dec_offsets.reshape(-1, BLOCK)
    outs = [enc_weights[2], mesh_weights[0, 2], mesh_weights[1, 2], dec_weights[2]]
    outs_other = [swap(outs[0])]
    gains = [enc_gain[None, :], mesh_gain]
    gains_other = [swap(x) for x in gains]
    halves = math.gcd(HALVES, chunks)
    xm = jnp.split(mesh_latent, halves)
    xt = jnp.split(swap(mesh_latent), halves)
    take = project(core, xm, xt, enc_weights[1], enc_bias[None, :])
    arrived, prepared, take, outs_other, gains_other, xm, xt = tie(
        arrived, prepared, take, outs_other, gains_other, xm, xt
    )
    gains = [gains[0], gains[1][:1], gains[1][1:]]
    gains_other = [gains_other[0], gains_other[1][:1], gains_other[1][1:]]
    e_list, m_list, d_list, counts, e_w, m_w, d_w = prepared
    length = list_length(mesh_send_block.shape[0])

    arrived_other = swap(arrived)
    nothing = jnp.zeros((1, columns), F32)
    send = project(core, [arrived], [arrived_other], enc_weights[0], nothing)
    agg = edge_sum(0, 0, counts, e_list, [send], take, e_off, e_w, None, halves)
    grid_take = project(core, [arrived], [arrived_other], dec_weights[1], dec_bias[None, :])
    for r in range(ROUNDS):
        xm, xt, send = mix_halves(
            chunks,
            False,
            core,
            agg,
            xm,
            xt,
            outs[r],
            outs_other[r],
            gains[r],
            gains_other[r],
            mesh_weights[r, 0],
        )
        near = [ring(x, to_near) for x in send]
        take = project(core, xm, xt, mesh_weights[r, 1], mesh_bias[r][None, :])
        common = (take, m_off, m_w)
        total = None
        far = []
        for k in range(chunks):
            if total is None:
                near[k], take = tie(near[k], take)
                common = (take, m_off, m_w)
            else:
                near[k], total = tie(near[k], total)
            far.append(ring(near[k], onward))
            if k < own_parts(chunks):
                total = edge_sum(
                    5 + k,
                    (3 + k) * length,
                    counts,
                    m_list,
                    send,
                    *common,
                    total,
                    0,
                )
        last_round = r + 1 == ROUNDS
        sources = [(mesh_weights, (r, 2))] + [(dec_weights, (2,))] * last_round
        arrays, total = tie([w for w, _ in sources], total)
        fresh = [swap(w[index]) for w, (_, index) in zip(arrays, sources)]
        total = edge_sum(2, 0, counts, m_list, near, *common, total, 0)
        total, fresh = tie(total, fresh)
        outs_other += fresh
        if chunks > 1:
            total = edge_sum(3, length, counts, m_list, far[:-1], *common, total, 0)
        agg = edge_sum(4, 2 * length, counts, m_list, far[-1:], *common, total, halves)
    xm, _, send = mix_halves(
        chunks,
        True,
        core,
        agg,
        xm,
        xt,
        outs[ROUNDS],
        outs_other[ROUNDS],
        gains[ROUNDS],
        gains_other[ROUNDS],
        dec_weights[0],
    )
    (agg,) = edge_sum(1, 0, counts, d_list, send, grid_take, d_off, d_w, None, 1)
    xm, agg = tie(xm, agg)
    other = swap(agg)
    mesh_out = joined_rows(xm)
    mesh_out, other = tie(mesh_out, other)
    update = update_of(core, agg, other, outs[3], outs_other[3], dec_gain[None, :])
    return place_rows(grid_order, exchange(update), grid_latent), mesh_out


def solution(mesh):
    in_specs = (
        P("nodes", "feat"),
        P("nodes", "feat"),
        P("nodes", None),
        P("nodes"),
        P("nodes"),
        P("nodes", None, None),
        P("nodes", None),
        P("nodes"),
        P("nodes"),
        P("nodes"),
        P("nodes", None, None),
        P("nodes", None),
        P("nodes"),
        P("nodes"),
        P("nodes"),
        P("nodes", None, None),
        P("nodes", None),
        P("nodes"),
        P(),
        P(None, None, "feat"),
        P(None, None, None, "feat"),
        P(None, None, "feat"),
        P("feat"),
        P("feat"),
        P(None, "feat"),
        P(None, "feat"),
        P("feat"),
        P("feat"),
    )
    out_specs = (P("nodes", "feat"), P("nodes", "feat"))
    return jax.shard_map(
        local, mesh=mesh, in_specs=in_specs, out_specs=out_specs, check_vma=False
    )
```

```python
import functools
import math

import jax
import jax.numpy as jnp
from jax import lax
from jax.experimental import pallas as pl
from jax.experimental.pallas import tpu as pltpu
from jax.sharding import PartitionSpec as P


BLOCK = 128
ROUNDS = 2
UNROLL = 4
CHUNKS = 4
HALVES = 2
EPSILON = 1e-05

VMEM = pl.BlockSpec(memory_space=pltpu.VMEM)
SMEM = pl.BlockSpec(memory_space=pltpu.SMEM)
HBM = pl.BlockSpec(memory_space=pltpu.HBM)
F32 = jnp.float32
BF16 = jnp.bfloat16


def dot(a, b):
    return jnp.dot(a, b, preferred_element_type=F32)


def params(mib=24):
    return pltpu.CompilerParams(vmem_limit_bytes=mib << 20)


def pieces(rows):
    return min(rows, 256)


def entry(slot, sender, taker, total):
    return slot + sender * 256 + taker * 65536 + total * 16777216


def list_length(slots):
    return slots + 2 * UNROLL


def own_parts(chunks):
    return max(chunks - 1, 1)


def spread_weights(labels, gains, index):
    marks = labels[...]
    weight = jnp.zeros(marks.shape, F32)
    for k in range(gains.shape[1]):
        weight = jnp.where(marks == k, gains[index, k], weight)
    return weight


def prepare_kernel(blocks, chunks, parity, *refs):
    inputs, refs = refs[:13], refs[13:]
    (e_list, m_list, d_list, counts, e_w, m_w, d_w), refs = refs[:7], refs[7:]
    held, sems = refs[:13], refs[13]
    copies = [
        pltpu.make_async_copy(source, target, sems.at[k])
        for k, (source, target) in enumerate(zip(inputs, held))
    ]
    for copy in copies:
        copy.start()
    for copy in copies:
        copy.wait()
    gains, es, er, el, ec, ms, mr, ml, mc, ds, dr, dl, dc = held

    def finish(out, base, count):
        for k in range(2 * UNROLL):
            out[base + count + k] = entry(0, 0, 0, blocks)
        return jnp.maximum((count + UNROLL - 1) // UNROLL, 1)

    def plain(sends, takes, live, out, where):
        total = live[0]

        def step(i, carry):
            taker = takes[i]
            out[i] = entry(i, sends[i], taker, taker)
            return carry

        lax.fori_loop(0, total, step, 0)
        counts[where] = finish(out, 0, total)

    plain(es, er, el, e_list, 0)
    plain(ds, dr, dl, d_list, 1)
    length = list_length(ms.shape[0])
    first = jnp.where(parity[0] == 0, 2, 0)
    last = 2 - first
    per = blocks // chunks

    def step(i, carry):
        sender = ms[i]
        taker = mr[i]
        group = sender // blocks
        inner = sender - group * blocks
        late = inner >= blocks - per
        inner = jnp.where((group == last) & late, inner - (blocks - per), inner)
        turn = carry[-1]
        which = jnp.where(
            group == 1, 3 + turn, jnp.where(group == first, 0, jnp.where(late, 2, 1))
        )
        place = carry[0]
        for k in range(1, lists):
            place = jnp.where(which == k, length * k + carry[k], place)
        m_list[place] = entry(i, inner, taker, taker)
        turn = jnp.where(group == 1, turn + 1, turn)
        turn = jnp.where(turn == lists - 3, 0, turn)
        counted = [c + (which == k).astype(jnp.int32) for k, c in enumerate(carry[:-1])]
        return (*counted, turn)

    lists = 3 + own_parts(chunks)
    zero = tuple(jnp.int32(0) for _ in range(lists + 1))
    found = lax.fori_loop(0, ml[0], step, zero)
    for k, count in enumerate(found[:-1]):
        counts[2 + k] = finish(m_list, length * k, count)

    for index, (labels, out) in enumerate(((ec, e_w), (mc, m_w), (dc, d_w))):
        out[...] = spread_weights(labels, gains, index)


def prepare(blocks, chunks, parity, gains, enc, mesh, dec):
    i32 = jnp.int32
    sets = (enc, mesh, dec)
    slots = [s[0].shape[0] for s in sets]
    sizes = [list_length(slots[0]), (3 + own_parts(chunks)) * list_length(slots[1])]
    sizes += [list_length(slots[2]), 8 + chunks]
    out_shape = [jax.ShapeDtypeStruct((n,), i32) for n in sizes]
    out_shape += [jax.ShapeDtypeStruct((n, BLOCK), F32) for n in slots]
    arrays = [gains, *enc, *mesh, *dec]
    spaces = [pltpu.SMEM] + [pltpu.SMEM, pltpu.SMEM, pltpu.SMEM, pltpu.VMEM] * 3
    scratch = [space(x.shape, x.dtype) for space, x in zip(spaces, arrays)]
    scratch.append(pltpu.SemaphoreType.DMA((len(arrays),)))
    return pl.pallas_call(
        functools.partial(prepare_kernel, blocks, chunks),
        out_shape=out_shape,
        in_specs=[SMEM] + [HBM] * len(arrays),
        out_specs=[SMEM] * 4 + [VMEM] * 3,
        scratch_shapes=scratch,
        compiler_params=params(4),
        cost_estimate=pl.CostEstimate(
            flops=2_000_000_000, bytes_accessed=1_000_000, transcendentals=0
        ),
    )(parity, *arrays)


def edge_loop(base, trips, items, send, take, offsets, weights, acc, picks, held):
    rows = lax.broadcasted_iota(jnp.int32, (BLOCK, BLOCK), 0).astype(F32).astype(BF16)
    one = jnp.ones((BLOCK, BLOCK), BF16)
    nil = jnp.zeros((BLOCK, BLOCK), BF16)

    def spread(row):
        return jnp.broadcast_to(row.astype(F32).astype(BF16), (BLOCK, BLOCK))

    def build(i):
        for u in range(UNROLL):
            slot = items[base + i * UNROLL + u] & 255
            both = [
                jnp.where(rows == spread(offsets[pl.ds(2 * slot + k, 1), :]), one, nil)
                for k in range(2)
            ]
            picks[u] = jnp.concatenate([x.T for x in both], axis=1)

    def gather(i):
        for u in range(UNROLL):
            item = items[base + i * UNROLL + u]
            sender = pl.multiple_of(((item >> 8) & 255) * BLOCK, BLOCK)
            taker = pl.multiple_of(((item >> 16) & 255) * BLOCK, BLOCK)
            both = jnp.concatenate(
                [send[pl.ds(sender, BLOCK), :], take[pl.ds(taker, BLOCK), :]], axis=0
            )
            half = dot(picks[u], both)
            held[u] = (half + half * jnp.tanh(half)).astype(BF16)

    def scatter(i):
        for u in range(UNROLL):
            item = items[base + i * UNROLL + u]
            slot = item & 255
            total = pl.multiple_of((item >> 24) * BLOCK, BLOCK)
            is_to = rows == spread(offsets[pl.ds(2 * slot + 1, 1), :])
            put = jnp.where(is_to, spread(weights[pl.ds(slot, 1), :]), nil)
            acc[pl.ds(total, BLOCK), :] += dot(put, held[u])

    def turn(i, carry):
        scatter(i - 1)
        gather(i)
        build(i + 1)
        return carry

    build(0)
    gather(0)
    build(1)
    lax.fori_loop(1, trips, turn, 0)
    scatter(trips - 1)


def edge_kernel(where, base, pieces_in, halves, first, counts, items, *refs):
    last = halves > 0
    refs = list(refs)
    sends = [refs.pop(0) for _ in range(pieces_in)]
    take, offsets, weights = refs[:3]
    refs = refs[3:]
    if not first:
        refs.pop(0)
    own_total = first and last
    count = halves + (not own_total)
    outs, refs = refs[:count], refs[count:]
    picks, held = refs[:2]
    refs = refs[2:]
    acc = refs.pop(0) if own_total else outs[halves]
    if first:
        acc[...] = jnp.zeros_like(acc)
    send = sends[0]
    if pieces_in > 1:
        joined = refs.pop(0)
        depth = send.shape[0]
        for k, piece in enumerate(sends):
            joined[pl.ds(k * depth, depth), :] = piece[...]
        send = joined
    edge_loop(base, counts[where], items, send, take, offsets, weights, acc, picks, held)
    for k, out in enumerate(outs[:halves]):
        depth = out.shape[0]
        out[...] = acc[pl.ds(k * depth, depth), :].astype(out.dtype)


def edge_sum(where, base, counts, items, sends, take, offsets, weights, before, halves):
    last = halves > 0
    first = before is None
    rows, columns = take.shape
    arrays = [counts, items, *sends, take, offsets, weights]
    aliases = {}
    if not first:
        aliases = {len(arrays): halves}
        arrays.append(before)
    full = (rows + BLOCK, columns)
    scratch = [
        pltpu.VMEM((UNROLL, BLOCK, width), BF16) for width in (2 * BLOCK, columns)
    ]
    shape = [jax.ShapeDtypeStruct((rows // max(halves, 1), columns), BF16)] * halves
    if first and last:
        scratch.append(pltpu.VMEM(full, F32))
    else:
        shape.append(jax.ShapeDtypeStruct(full, F32))
    if len(sends) > 1:
        depth = sum(x.shape[0] for x in sends)
        scratch.append(pltpu.VMEM((depth, columns), BF16))
    result = pl.pallas_call(
        functools.partial(edge_kernel, where, base, len(sends), halves, first),
        out_shape=shape,
        in_specs=[SMEM, SMEM] + [VMEM] * (len(arrays) - 2),
        out_specs=[VMEM] * len(shape),
        scratch_shapes=scratch,
        input_output_aliases=aliases,
        compiler_params=params(),
        cost_estimate=pl.CostEstimate(
            flops=2_000_000_000, bytes_accessed=2_000_000, transcendentals=1_000_000
        ),
    )(*arrays)
    return list(result[:halves]) if last else result[0]


def two_dots(a, b, weights, mine, other, width):
    return dot(a, weights[pl.ds(mine, width), :]) + dot(b, weights[pl.ds(other, width), :])


def normalized(ym, yt):
    width = ym.shape[1] + yt.shape[1]
    total = jnp.sum(ym + yt, axis=1, keepdims=True)
    squares = jnp.sum(ym * ym + yt * yt, axis=1, keepdims=True)
    mean = total / width
    spread = squares / width - mean * mean
    return mean, lax.rsqrt(spread + EPSILON)


def mix_kernel(
    chunks, core, am, at, xm, xt, wm, wt, gm, gt, ws, out_m, *outs
):
    rows, width = am.shape
    out_s, out_t = outs[:chunks], outs[chunks:]
    tile = rows // chunks
    mine = pl.multiple_of(core[0] * width, width)
    other = pl.multiple_of(width - core[0] * width, width)

    for t in range(rows // tile):
        part = pl.ds(t * tile, tile)
        a = am[part, :]
        b = at[part, :]
        ym = two_dots(a, b, wm, mine, other, width)
        yt = two_dots(a, b, wt, mine, other, width)
        mean, scale = normalized(ym, yt)
        nm = (xm[part, :].astype(F32) + (ym - mean) * scale * gm[...]).astype(BF16)
        nt = (xt[part, :].astype(F32) + (yt - mean) * scale * gt[...]).astype(BF16)
        out_m[part, :] = nm
        for out in out_t:
            out[part, :] = nt
        out_s[t][...] = (0.5 * two_dots(nm, nt, ws, mine, other, width)).astype(BF16)


def mix(chunks, last, core, am, at, xm, xt, wm, wt, gm, gt, ws):
    rows, width = am.shape
    shapes = [jax.ShapeDtypeStruct((rows, width), BF16)]
    shapes += [jax.ShapeDtypeStruct((rows // chunks, width), BF16)] * chunks
    shapes += shapes[:1] * (not last)
    new_xm, *rest = pl.pallas_call(
        functools.partial(mix_kernel, chunks),
        out_shape=shapes,
        in_specs=[SMEM] + [VMEM] * 9,
        out_specs=[VMEM] * len(shapes),
        compiler_params=params(),
    )(core, am, at, xm, xt, wm, wt, gm, gt, ws)
    return new_xm, rest[:chunks], rest[chunks:]


def mix_halves(chunks, last, core, aggs, xms, xts, *rest):
    others = [swap(x) for x in aggs]
    results = [
        mix(chunks // len(aggs), last, core, am, at, xm, xt, *rest)
        for am, at, xm, xt in zip(aggs, others, xms, xts)
    ]
    send = [x for _, part, _ in results for x in part]
    return [x for x, _, _ in results], [x for _, _, t in results for x in t], send


def copy_kernel(*refs):
    ins, out = refs[:-1], refs[-1]
    depth = ins[0].shape[0]
    for k, x in enumerate(ins):
        out[pl.ds(k * depth, depth), :] = x[...]


def joined_rows(xs):
    rows, width = xs[0].shape
    return pl.pallas_call(
        copy_kernel,
        out_shape=jax.ShapeDtypeStruct((rows * len(xs), width), BF16),
        in_specs=[VMEM] * len(xs),
        out_specs=VMEM,
        compiler_params=params(4),
    )(*xs)


def project_kernel(core, *refs):
    w, bias, out = refs[-3:]
    parts = len(refs[:-3]) // 2
    depth, width = refs[0].shape
    rows = depth * parts
    tile = pieces(depth)
    mine = pl.multiple_of(core[0] * width, width)
    other = pl.multiple_of(width - core[0] * width, width)

    for t in range(rows // tile):
        part = pl.ds(t * tile, tile)
        which, inner = divmod(t * tile, depth)
        inner = pl.ds(inner, tile)
        xm, xt = refs[which], refs[parts + which]
        y = two_dots(xm[inner, :], xt[inner, :], w, mine, other, width)
        out[part, :] = (0.5 * (y + bias[...])).astype(BF16)


def project(core, xm, xt, w, bias):
    rows, width = xm[0].shape
    return pl.pallas_call(
        project_kernel,
        out_shape=jax.ShapeDtypeStruct((rows * len(xm), width), BF16),
        in_specs=[SMEM] + [VMEM] * (2 * len(xm) + 2),
        out_specs=VMEM,
        compiler_params=params(),
    )(core, *xm, *xt, w, bias)


def update_kernel(core, am, at, wm, wt, gm, out):
    rows, width = am.shape
    tile = pieces(rows)
    mine = pl.multiple_of(core[0] * width, width)
    other = pl.multiple_of(width - core[0] * width, width)

    for t in range(rows // tile):
        part = pl.ds(t * tile, tile)
        a = am[part, :]
        b = at[part, :]
        ym = two_dots(a, b, wm, mine, other, width)
        yt = two_dots(a, b, wt, mine, other, width)
        mean, scale = normalized(ym, yt)
        out[part, :] = ((ym - mean) * scale * gm[...]).astype(BF16)


def update_of(core, am, at, wm, wt, gm):
    return pl.pallas_call(
        update_kernel,
        out_shape=jax.ShapeDtypeStruct(am.shape, BF16),
        in_specs=[SMEM] + [VMEM] * 5,
        out_specs=VMEM,
        compiler_params=params(),
    )(core, am, at, wm, wt, gm)


def pick_rows_kernel(order_in, x_in, out, order, x, sems):
    copies = [
        pltpu.make_async_copy(order_in, order, sems.at[0]),
        pltpu.make_async_copy(x_in, x, sems.at[1]),
    ]
    for copy in copies:
        copy.start()
    for copy in copies:
        copy.wait()
    rows = x.shape[0]
    tile = pieces(rows)
    for t in range(rows // tile):
        part = pl.ds(t * tile, tile)
        ids = lax.broadcasted_iota(jnp.int32, (rows, tile), 0)
        chosen = jnp.where(ids == order[:, part], 1.0, 0.0).astype(BF16)
        out[part, :] = lax.dot_general(
            chosen, x[...], (((0,), (0,)), ((), ())), preferred_element_type=F32
        ).astype(BF16)


def pick_rows(order, x):
    return pl.pallas_call(
        pick_rows_kernel,
        out_shape=jax.ShapeDtypeStruct(x.shape, BF16),
        in_specs=[HBM] * 2,
        out_specs=VMEM,
        scratch_shapes=[
            pltpu.VMEM(order.shape, order.dtype),
            pltpu.VMEM(x.shape, x.dtype),
            pltpu.SemaphoreType.DMA((2,)),
        ],
        compiler_params=params(62),
    )(order, x)


def place_rows_kernel(order, x, rest, out):
    rows = x.shape[0]
    tile = pieces(rows)

    for t in range(rows // tile):
        start = t * tile
        part = pl.ds(start, tile)
        ids = lax.broadcasted_iota(jnp.int32, (tile, rows), 0) + start
        chosen = jnp.where(ids == order[...], 1.0, 0.0).astype(BF16)
        out[part, :] = (rest[part, :].astype(F32) + dot(chosen, x[...])).astype(BF16)


def place_rows(order, x, rest):
    return pl.pallas_call(
        place_rows_kernel,
        out_shape=jax.ShapeDtypeStruct(x.shape, BF16),
        in_specs=[VMEM] * 3,
        out_specs=VMEM,
        compiler_params=params(),
    )(order, x, rest)


def swap(x):
    return lax.ppermute(x, "feat", [(0, 1), (1, 0)])


def exchange(x):
    return lax.all_to_all(x, "nodes", split_axis=0, concat_axis=0, tiled=True)


def tie(*values):
    return lax.optimization_barrier(values)


def ring(chunk, pairs):
    return lax.ppermute(chunk, "nodes", pairs)


def local(
    grid_latent,
    mesh_latent,
    grid_order,
    enc_send_block,
    enc_recv_block,
    enc_offsets,
    enc_classes,
    enc_live,
    mesh_send_block,
    mesh_recv_block,
    mesh_offsets,
    mesh_classes,
    mesh_live,
    dec_send_block,
    dec_recv_block,
    dec_offsets,
    dec_classes,
    dec_live,
    class_gain,
    enc_weights,
    mesh_weights,
    dec_weights,
    enc_bias,
    enc_gain,
    mesh_bias,
    mesh_gain,
    dec_bias,
    dec_gain,
):
    rows, columns = mesh_latent.shape
    size = lax.axis_size("nodes")
    to_near = [(j, j ^ 1) for j in range(size)]
    onward = [(j, (j + 2 - 4 * (j % 2)) % size) for j in range(size)]
    core = lax.axis_index("feat").astype(jnp.int32).reshape(1)
    parity = (lax.axis_index("nodes") % 2).astype(jnp.int32).reshape(1)
    arrived = exchange(pick_rows(grid_order, grid_latent))

    chunks = math.gcd(CHUNKS, rows // BLOCK)
    prepared = prepare(
        rows // BLOCK,
        chunks,
        parity,
        class_gain,
        (enc_send_block, enc_recv_block, enc_live, enc_classes),
        (mesh_send_block, mesh_recv_block, mesh_live, mesh_classes),
        (dec_send_block, dec_recv_block, dec_live, dec_classes),
    )
    e_off = enc_offsets.reshape(-1, BLOCK)
    m_off = mesh_offsets.reshape(-1, BLOCK)
    d_off = dec_offsets.reshape(-1, BLOCK)
    outs = [enc_weights[2], mesh_weights[0, 2], mesh_weights[1, 2], dec_weights[2]]
    outs_other = [swap(outs[0])]
    gains = [enc_gain[None, :], mesh_gain]
    gains_other = [swap(x) for x in gains]
    halves = math.gcd(HALVES, chunks)
    xm = jnp.split(mesh_latent, halves)
    xt = jnp.split(swap(mesh_latent), halves)
    take = project(core, xm, xt, enc_weights[1], enc_bias[None, :])
    arrived, prepared, take, outs_other, gains_other, xm, xt = tie(
        arrived, prepared, take, outs_other, gains_other, xm, xt
    )
    gains = [gains[0], gains[1][:1], gains[1][1:]]
    gains_other = [gains_other[0], gains_other[1][:1], gains_other[1][1:]]
    e_list, m_list, d_list, counts, e_w, m_w, d_w = prepared
    length = list_length(mesh_send_block.shape[0])

    arrived_other = swap(arrived)
    nothing = jnp.zeros((1, columns), F32)
    send = project(core, [arrived], [arrived_other], enc_weights[0], nothing)
    agg = edge_sum(0, 0, counts, e_list, [send], take, e_off, e_w, None, halves)
    grid_take = project(core, [arrived], [arrived_other], dec_weights[1], dec_bias[None, :])
    for r in range(ROUNDS):
        xm, xt, send = mix_halves(
            chunks,
            False,
            core,
            agg,
            xm,
            xt,
            outs[r],
            outs_other[r],
            gains[r],
            gains_other[r],
            mesh_weights[r, 0],
        )
        near = [ring(x, to_near) for x in send]
        take = project(core, xm, xt, mesh_weights[r, 1], mesh_bias[r][None, :])
        common = (take, m_off, m_w)
        total = None
        far = []
        for k in range(chunks):
            if total is None:
                near[k], take = tie(near[k], take)
                common = (take, m_off, m_w)
            else:
                near[k], total = tie(near[k], total)
            far.append(ring(near[k], onward))
            if k < own_parts(chunks):
                total = edge_sum(
                    5 + k,
                    (3 + k) * length,
                    counts,
                    m_list,
                    send,
                    *common,
                    total,
                    0,
                )
        total = edge_sum(2, 0, counts, m_list, near, *common, total, 0)
        last_round = r + 1 == ROUNDS
        sources = [(mesh_weights, (r, 2))] + [(dec_weights, (2,))] * last_round
        arrays, total = tie([w for w, _ in sources], total)
        fresh = [swap(w[index]) for w, (_, index) in zip(arrays, sources)]
        if chunks > 1:
            total = edge_sum(3, length, counts, m_list, far[:-1], *common, total, 0)
        total, fresh = tie(total, fresh)
        outs_other += fresh
        agg = edge_sum(4, 2 * length, counts, m_list, far[-1:], *common, total, halves)
    xm, _, send = mix_halves(
        chunks,
        True,
        core,
        agg,
        xm,
        xt,
        outs[ROUNDS],
        outs_other[ROUNDS],
        gains[ROUNDS],
        gains_other[ROUNDS],
        dec_weights[0],
    )
    (agg,) = edge_sum(1, 0, counts, d_list, send, grid_take, d_off, d_w, None, 1)
    xm, agg = tie(xm, agg)
    other = swap(agg)
    mesh_out = joined_rows(xm)
    mesh_out, other = tie(mesh_out, other)
    update = update_of(core, agg, other, outs[3], outs_other[3], dec_gain[None, :])
    return place_rows(grid_order, exchange(update), grid_latent), mesh_out


def solution(mesh):
    in_specs = (
        P("nodes", "feat"),
        P("nodes", "feat"),
        P("nodes", None),
        P("nodes"),
        P("nodes"),
        P("nodes", None, None),
        P("nodes", None),
        P("nodes"),
        P("nodes"),
        P("nodes"),
        P("nodes", None, None),
        P("nodes", None),
        P("nodes"),
        P("nodes"),
        P("nodes"),
        P("nodes", None, None),
        P("nodes", None),
        P("nodes"),
        P(),
        P(None, None, "feat"),
        P(None, None, None, "feat"),
        P(None, None, "feat"),
        P("feat"),
        P("feat"),
        P(None, "feat"),
        P(None, "feat"),
        P("feat"),
        P("feat"),
    )
    out_specs = (P("nodes", "feat"), P("nodes", "feat"))
    return jax.shard_map(
        local, mesh=mesh, in_specs=in_specs, out_specs=out_specs, check_vma=False
    )
```

```python
import functools
import itertools
import math

import jax
import jax.numpy as jnp
from jax import lax
from jax.experimental import pallas as pl
from jax.experimental.pallas import tpu as pltpu
from jax.sharding import PartitionSpec as P


BLOCK = 128
ROUNDS = 2
UNROLL = 4
CHUNKS = 4
EPSILON = 1e-05

VMEM = pl.BlockSpec(memory_space=pltpu.VMEM)
SMEM = pl.BlockSpec(memory_space=pltpu.SMEM)
HBM = pl.BlockSpec(memory_space=pltpu.HBM)
F32 = jnp.float32
BF16 = jnp.bfloat16


def dot(a, b):
    return jnp.dot(a, b, preferred_element_type=F32)


def params(mib=24):
    return pltpu.CompilerParams(vmem_limit_bytes=mib << 20)


def pieces(rows):
    return min(rows, 256)


def entry(slot, sender, taker, total):
    return slot + sender * 256 + taker * 65536 + total * 16777216


def list_length(slots):
    return slots + 2 * UNROLL


def part_chunks(chunks):
    return (1, 1, chunks - 2) if chunks > 2 else (chunks,)


def own_parts(chunks):
    return max(chunks - 1, 1)


def spread_weights(labels, gains, index):
    marks = labels[...]
    weight = jnp.zeros(marks.shape, F32)
    for k in range(gains.shape[1]):
        weight = jnp.where(marks == k, gains[index, k], weight)
    return weight


def prepare_kernel(blocks, chunks, parity, *refs):
    inputs, refs = refs[:13], refs[13:]
    (e_list, m_list, d_list, counts, e_w, m_w, d_w), refs = refs[:7], refs[7:]
    held, sems = refs[:13], refs[13]
    copies = [
        pltpu.make_async_copy(source, target, sems.at[k])
        for k, (source, target) in enumerate(zip(inputs, held))
    ]
    for copy in copies:
        copy.start()
    for copy in copies:
        copy.wait()
    gains, es, er, el, ec, ms, mr, ml, mc, ds, dr, dl, dc = held

    def finish(out, base, count):
        for k in range(2 * UNROLL):
            out[base + count + k] = entry(0, 0, 0, blocks)
        return jnp.maximum((count + UNROLL - 1) // UNROLL, 1)

    def plain(sends, takes, live, out, where):
        total = live[0]

        def step(i, carry):
            taker = takes[i]
            out[i] = entry(i, sends[i], taker, taker)
            return carry

        lax.fori_loop(0, total, step, 0)
        counts[where] = finish(out, 0, total)

    plain(es, er, el, e_list, 0)
    plain(ds, dr, dl, d_list, 1)
    length = list_length(ms.shape[0])
    first = jnp.where(parity[0] == 0, 2, 0)
    last = 2 - first
    per = blocks // chunks

    def step(i, carry):
        sender = ms[i]
        taker = mr[i]
        group = sender // blocks
        inner = sender - group * blocks
        late = inner >= blocks - per
        inner = jnp.where((group == last) & late, inner - (blocks - per), inner)
        turn = carry[-1]
        which = jnp.where(
            group == 1, 3 + turn, jnp.where(group == first, 0, jnp.where(late, 2, 1))
        )
        place = carry[0]
        for k in range(1, lists):
            place = jnp.where(which == k, length * k + carry[k], place)
        m_list[place] = entry(i, inner, taker, taker)
        turn = jnp.where(group == 1, turn + 1, turn)
        turn = jnp.where(turn == lists - 3, 0, turn)
        counted = [c + (which == k).astype(jnp.int32) for k, c in enumerate(carry[:-1])]
        return (*counted, turn)

    lists = 3 + own_parts(chunks)
    zero = tuple(jnp.int32(0) for _ in range(lists + 1))
    found = lax.fori_loop(0, ml[0], step, zero)
    for k, count in enumerate(found[:-1]):
        counts[2 + k] = finish(m_list, length * k, count)

    for index, (labels, out) in enumerate(((ec, e_w), (mc, m_w), (dc, d_w))):
        out[...] = spread_weights(labels, gains, index)


def prepare(blocks, chunks, parity, gains, enc, mesh, dec):
    i32 = jnp.int32
    sets = (enc, mesh, dec)
    slots = [s[0].shape[0] for s in sets]
    sizes = [list_length(slots[0]), (3 + own_parts(chunks)) * list_length(slots[1])]
    sizes += [list_length(slots[2]), 8 + chunks]
    out_shape = [jax.ShapeDtypeStruct((n,), i32) for n in sizes]
    out_shape += [jax.ShapeDtypeStruct((n, BLOCK), F32) for n in slots]
    arrays = [gains, *enc, *mesh, *dec]
    spaces = [pltpu.SMEM] + [pltpu.SMEM, pltpu.SMEM, pltpu.SMEM, pltpu.VMEM] * 3
    scratch = [space(x.shape, x.dtype) for space, x in zip(spaces, arrays)]
    scratch.append(pltpu.SemaphoreType.DMA((len(arrays),)))
    return pl.pallas_call(
        functools.partial(prepare_kernel, blocks, chunks),
        out_shape=out_shape,
        in_specs=[SMEM] + [HBM] * len(arrays),
        out_specs=[SMEM] * 4 + [VMEM] * 3,
        scratch_shapes=scratch,
        compiler_params=params(4),
        cost_estimate=pl.CostEstimate(
            flops=2_000_000_000, bytes_accessed=1_000_000, transcendentals=0
        ),
    )(parity, *arrays)


def edge_loop(base, trips, items, send, take, offsets, weights, acc, picks, held):
    rows = lax.broadcasted_iota(jnp.int32, (BLOCK, BLOCK), 0).astype(F32).astype(BF16)
    one = jnp.ones((BLOCK, BLOCK), BF16)
    nil = jnp.zeros((BLOCK, BLOCK), BF16)

    def spread(row):
        return jnp.broadcast_to(row.astype(F32).astype(BF16), (BLOCK, BLOCK))

    def build(i):
        for u in range(UNROLL):
            slot = items[base + i * UNROLL + u] & 255
            both = [
                jnp.where(rows == spread(offsets[pl.ds(2 * slot + k, 1), :]), one, nil)
                for k in range(2)
            ]
            picks[u] = jnp.concatenate([x.T for x in both], axis=1)

    def gather(i):
        for u in range(UNROLL):
            item = items[base + i * UNROLL + u]
            sender = pl.multiple_of(((item >> 8) & 255) * BLOCK, BLOCK)
            taker = pl.multiple_of(((item >> 16) & 255) * BLOCK, BLOCK)
            both = jnp.concatenate(
                [send[pl.ds(sender, BLOCK), :], take[pl.ds(taker, BLOCK), :]], axis=0
            )
            half = dot(picks[u], both)
            held[u] = (half + half * jnp.tanh(half)).astype(BF16)

    def scatter(i):
        for u in range(UNROLL):
            item = items[base + i * UNROLL + u]
            slot = item & 255
            total = pl.multiple_of((item >> 24) * BLOCK, BLOCK)
            is_to = rows == spread(offsets[pl.ds(2 * slot + 1, 1), :])
            put = jnp.where(is_to, spread(weights[pl.ds(slot, 1), :]), nil)
            acc[pl.ds(total, BLOCK), :] += dot(put, held[u])

    def turn(i, carry):
        scatter(i - 1)
        gather(i)
        build(i + 1)
        return carry

    build(0)
    gather(0)
    build(1)
    lax.fori_loop(1, trips, turn, 0)
    scatter(trips - 1)


def edge_kernel(where, base, pieces_in, halves, first, counts, items, *refs):
    last = halves > 0
    place = 0
    refs = list(refs)
    sends = [refs.pop(0) for _ in range(pieces_in)]
    take, offsets, weights = refs[:3]
    refs = refs[3:]
    if not first:
        refs.pop(0)
    own_total = first and last
    count = halves + (not own_total)
    outs, refs = refs[:count], refs[count:]
    picks, held = refs[:2]
    refs = refs[2:]
    acc = refs.pop(0) if own_total else outs[halves]
    if first:
        acc[...] = jnp.zeros_like(acc)
    send = sends[0]
    if pieces_in > 1:
        joined = refs.pop(0)
        depth = send.shape[0]
        for k, piece in enumerate(sends):
            joined[pl.ds(k * depth, depth), :] = piece[...]
        send = joined
    edge_loop(base, counts[where], items, send, take, offsets, weights, acc, picks, held)
    for out in outs[:halves]:
        depth = out.shape[0]
        out[...] = acc[pl.ds(place, depth), :].astype(out.dtype)
        place += depth


def edge_sum(where, base, counts, items, sends, take, offsets, weights, before, parts):
    halves = len(parts)
    last = halves > 0
    first = before is None
    rows, columns = take.shape
    arrays = [counts, items, *sends, take, offsets, weights]
    aliases = {}
    if not first:
        aliases = {len(arrays): halves}
        arrays.append(before)
    full = (rows + BLOCK, columns)
    scratch = [
        pltpu.VMEM((UNROLL, BLOCK, width), BF16) for width in (2 * BLOCK, columns)
    ]
    shape = [jax.ShapeDtypeStruct((n, columns), BF16) for n in parts]
    if first and last:
        scratch.append(pltpu.VMEM(full, F32))
    else:
        shape.append(jax.ShapeDtypeStruct(full, F32))
    if len(sends) > 1:
        depth = sum(x.shape[0] for x in sends)
        scratch.append(pltpu.VMEM((depth, columns), BF16))
    result = pl.pallas_call(
        functools.partial(edge_kernel, where, base, len(sends), halves, first),
        out_shape=shape,
        in_specs=[SMEM, SMEM] + [VMEM] * (len(arrays) - 2),
        out_specs=[VMEM] * len(shape),
        scratch_shapes=scratch,
        input_output_aliases=aliases,
        compiler_params=params(),
        cost_estimate=pl.CostEstimate(
            flops=2_000_000_000, bytes_accessed=2_000_000, transcendentals=1_000_000
        ),
    )(*arrays)
    return list(result[:halves]) if last else result[0]


def two_dots(a, b, weights, mine, other, width):
    return dot(a, weights[pl.ds(mine, width), :]) + dot(b, weights[pl.ds(other, width), :])


def normalized(ym, yt):
    width = ym.shape[1] + yt.shape[1]
    total = jnp.sum(ym + yt, axis=1, keepdims=True)
    squares = jnp.sum(ym * ym + yt * yt, axis=1, keepdims=True)
    mean = total / width
    spread = squares / width - mean * mean
    return mean, lax.rsqrt(spread + EPSILON)


def mix_kernel(
    chunks, core, am, at, xm, xt, wm, wt, gm, gt, ws, out_m, *outs
):
    rows, width = am.shape
    out_s, out_t = outs[:chunks], outs[chunks:]
    tile = rows // chunks
    mine = pl.multiple_of(core[0] * width, width)
    other = pl.multiple_of(width - core[0] * width, width)

    for t in range(rows // tile):
        part = pl.ds(t * tile, tile)
        a = am[part, :]
        b = at[part, :]
        ym = two_dots(a, b, wm, mine, other, width)
        yt = two_dots(a, b, wt, mine, other, width)
        mean, scale = normalized(ym, yt)
        nm = (xm[part, :].astype(F32) + (ym - mean) * scale * gm[...]).astype(BF16)
        nt = (xt[part, :].astype(F32) + (yt - mean) * scale * gt[...]).astype(BF16)
        out_m[part, :] = nm
        for out in out_t:
            out[part, :] = nt
        out_s[t][...] = (0.5 * two_dots(nm, nt, ws, mine, other, width)).astype(BF16)


def mix(chunks, last, core, am, at, xm, xt, wm, wt, gm, gt, ws):
    rows, width = am.shape
    shapes = [jax.ShapeDtypeStruct((rows, width), BF16)]
    shapes += [jax.ShapeDtypeStruct((rows // chunks, width), BF16)] * chunks
    shapes += shapes[:1] * (not last)
    new_xm, *rest = pl.pallas_call(
        functools.partial(mix_kernel, chunks),
        out_shape=shapes,
        in_specs=[SMEM] + [VMEM] * 9,
        out_specs=[VMEM] * len(shapes),
        compiler_params=params(),
    )(core, am, at, xm, xt, wm, wt, gm, gt, ws)
    return new_xm, rest[:chunks], rest[chunks:]


def mix_halves(chunks, last, core, aggs, xms, xts, *rest):
    others = [swap(x) for x in aggs]
    results = [
        mix(n, last, core, am, at, xm, xt, *rest)
        for n, am, at, xm, xt in zip(part_chunks(chunks), aggs, others, xms, xts)
    ]
    send = [x for _, part, _ in results for x in part]
    return [x for x, _, _ in results], [x for _, _, t in results for x in t], send


def copy_kernel(*refs):
    ins, out = refs[:-1], refs[-1]
    place = 0
    for x in ins:
        out[pl.ds(place, x.shape[0]), :] = x[...]
        place += x.shape[0]


def joined_rows(xs):
    rows, width = sum(x.shape[0] for x in xs), xs[0].shape[1]
    return pl.pallas_call(
        copy_kernel,
        out_shape=jax.ShapeDtypeStruct((rows, width), BF16),
        in_specs=[VMEM] * len(xs),
        out_specs=VMEM,
        compiler_params=params(4),
    )(*xs)


def project_kernel(core, *refs):
    w, bias, out = refs[-3:]
    parts = len(refs[:-3]) // 2
    width = refs[0].shape[1]
    depths = [x.shape[0] for x in refs[:parts]]
    tile = min(pieces(n) for n in depths)
    spots = [(k, a) for k, n in enumerate(depths) for a in range(0, n, tile)]
    mine = pl.multiple_of(core[0] * width, width)
    other = pl.multiple_of(width - core[0] * width, width)

    for t, (which, start) in enumerate(spots):
        part = pl.ds(t * tile, tile)
        inner = pl.ds(start, tile)
        xm, xt = refs[which], refs[parts + which]
        y = two_dots(xm[inner, :], xt[inner, :], w, mine, other, width)
        out[part, :] = (0.5 * (y + bias[...])).astype(BF16)


def project(core, xm, xt, w, bias):
    rows, width = sum(x.shape[0] for x in xm), xm[0].shape[1]
    return pl.pallas_call(
        project_kernel,
        out_shape=jax.ShapeDtypeStruct((rows, width), BF16),
        in_specs=[SMEM] + [VMEM] * (2 * len(xm) + 2),
        out_specs=VMEM,
        compiler_params=params(),
    )(core, *xm, *xt, w, bias)


def update_kernel(core, am, at, wm, wt, gm, out):
    rows, width = am.shape
    tile = pieces(rows)
    mine = pl.multiple_of(core[0] * width, width)
    other = pl.multiple_of(width - core[0] * width, width)

    for t in range(rows // tile):
        part = pl.ds(t * tile, tile)
        a = am[part, :]
        b = at[part, :]
        ym = two_dots(a, b, wm, mine, other, width)
        yt = two_dots(a, b, wt, mine, other, width)
        mean, scale = normalized(ym, yt)
        out[part, :] = ((ym - mean) * scale * gm[...]).astype(BF16)


def update_of(core, am, at, wm, wt, gm):
    return pl.pallas_call(
        update_kernel,
        out_shape=jax.ShapeDtypeStruct(am.shape, BF16),
        in_specs=[SMEM] + [VMEM] * 5,
        out_specs=VMEM,
        compiler_params=params(),
    )(core, am, at, wm, wt, gm)


def pick_rows_kernel(order_in, x_in, out, order, x, sems):
    copies = [
        pltpu.make_async_copy(order_in, order, sems.at[0]),
        pltpu.make_async_copy(x_in, x, sems.at[1]),
    ]
    for copy in copies:
        copy.start()
    for copy in copies:
        copy.wait()
    rows = x.shape[0]
    tile = pieces(rows)
    for t in range(rows // tile):
        part = pl.ds(t * tile, tile)
        ids = lax.broadcasted_iota(jnp.int32, (rows, tile), 0)
        chosen = jnp.where(ids == order[:, part], 1.0, 0.0).astype(BF16)
        out[part, :] = lax.dot_general(
            chosen, x[...], (((0,), (0,)), ((), ())), preferred_element_type=F32
        ).astype(BF16)


def pick_rows(order, x):
    return pl.pallas_call(
        pick_rows_kernel,
        out_shape=jax.ShapeDtypeStruct(x.shape, BF16),
        in_specs=[HBM] * 2,
        out_specs=VMEM,
        scratch_shapes=[
            pltpu.VMEM(order.shape, order.dtype),
            pltpu.VMEM(x.shape, x.dtype),
            pltpu.SemaphoreType.DMA((2,)),
        ],
        compiler_params=params(62),
    )(order, x)


def place_rows_kernel(order, x, rest, out):
    rows = x.shape[0]
    tile = pieces(rows)

    for t in range(rows // tile):
        start = t * tile
        part = pl.ds(start, tile)
        ids = lax.broadcasted_iota(jnp.int32, (tile, rows), 0) + start
        chosen = jnp.where(ids == order[...], 1.0, 0.0).astype(BF16)
        out[part, :] = (rest[part, :].astype(F32) + dot(chosen, x[...])).astype(BF16)


def place_rows(order, x, rest):
    return pl.pallas_call(
        place_rows_kernel,
        out_shape=jax.ShapeDtypeStruct(x.shape, BF16),
        in_specs=[VMEM] * 3,
        out_specs=VMEM,
        compiler_params=params(),
    )(order, x, rest)


def swap(x):
    return lax.ppermute(x, "feat", [(0, 1), (1, 0)])


def exchange(x):
    return lax.all_to_all(x, "nodes", split_axis=0, concat_axis=0, tiled=True)


def tie(*values):
    return lax.optimization_barrier(values)


def ring(chunk, pairs):
    return lax.ppermute(chunk, "nodes", pairs)


def local(
    grid_latent,
    mesh_latent,
    grid_order,
    enc_send_block,
    enc_recv_block,
    enc_offsets,
    enc_classes,
    enc_live,
    mesh_send_block,
    mesh_recv_block,
    mesh_offsets,
    mesh_classes,
    mesh_live,
    dec_send_block,
    dec_recv_block,
    dec_offsets,
    dec_classes,
    dec_live,
    class_gain,
    enc_weights,
    mesh_weights,
    dec_weights,
    enc_bias,
    enc_gain,
    mesh_bias,
    mesh_gain,
    dec_bias,
    dec_gain,
):
    rows, columns = mesh_latent.shape
    size = lax.axis_size("nodes")
    to_near = [(j, j ^ 1) for j in range(size)]
    onward = [(j, (j + 2 - 4 * (j % 2)) % size) for j in range(size)]
    core = lax.axis_index("feat").astype(jnp.int32).reshape(1)
    parity = (lax.axis_index("nodes") % 2).astype(jnp.int32).reshape(1)
    arrived = exchange(pick_rows(grid_order, grid_latent))

    chunks = math.gcd(CHUNKS, rows // BLOCK)
    prepared = prepare(
        rows // BLOCK,
        chunks,
        parity,
        class_gain,
        (enc_send_block, enc_recv_block, enc_live, enc_classes),
        (mesh_send_block, mesh_recv_block, mesh_live, mesh_classes),
        (dec_send_block, dec_recv_block, dec_live, dec_classes),
    )
    e_off = enc_offsets.reshape(-1, BLOCK)
    m_off = mesh_offsets.reshape(-1, BLOCK)
    d_off = dec_offsets.reshape(-1, BLOCK)
    outs = [enc_weights[2], mesh_weights[0, 2], mesh_weights[1, 2], dec_weights[2]]
    outs_other = [swap(outs[0])]
    gains = [enc_gain[None, :], mesh_gain]
    gains_other = [swap(x) for x in gains]
    parts = [n * (rows // chunks) for n in part_chunks(chunks)]
    cuts = list(itertools.accumulate(parts))[:-1]
    xm = jnp.split(mesh_latent, cuts)
    xt = jnp.split(swap(mesh_latent), cuts)
    take = project(core, xm, xt, enc_weights[1], enc_bias[None, :])
    arrived, prepared, take, outs_other, gains_other, xm, xt = tie(
        arrived, prepared, take, outs_other, gains_other, xm, xt
    )
    gains = [gains[0], gains[1][:1], gains[1][1:]]
    gains_other = [gains_other[0], gains_other[1][:1], gains_other[1][1:]]
    e_list, m_list, d_list, counts, e_w, m_w, d_w = prepared
    length = list_length(mesh_send_block.shape[0])

    arrived_other = swap(arrived)
    nothing = jnp.zeros((1, columns), F32)
    send = project(core, [arrived], [arrived_other], enc_weights[0], nothing)
    agg = edge_sum(0, 0, counts, e_list, [send], take, e_off, e_w, None, parts)
    grid_take = project(core, [arrived], [arrived_other], dec_weights[1], dec_bias[None, :])
    for r in range(ROUNDS):
        xm, xt, send = mix_halves(
            chunks,
            False,
            core,
            agg,
            xm,
            xt,
            outs[r],
            outs_other[r],
            gains[r],
            gains_other[r],
            mesh_weights[r, 0],
        )
        near = [ring(x, to_near) for x in send]
        take = project(core, xm, xt, mesh_weights[r, 1], mesh_bias[r][None, :])
        common = (take, m_off, m_w)
        total = None
        far = []
        for k in range(chunks):
            if total is None:
                near[k], take = tie(near[k], take)
                common = (take, m_off, m_w)
            else:
                near[k], total = tie(near[k], total)
            far.append(ring(near[k], onward))
            if k < own_parts(chunks):
                total = edge_sum(
                    5 + k,
                    (3 + k) * length,
                    counts,
                    m_list,
                    send,
                    *common,
                    total,
                    (),
                )
        total = edge_sum(2, 0, counts, m_list, near, *common, total, ())
        last_round = r + 1 == ROUNDS
        sources = [(mesh_weights, (r, 2))] + [(dec_weights, (2,))] * last_round
        arrays, total = tie([w for w, _ in sources], total)
        fresh = [swap(w[index]) for w, (_, index) in zip(arrays, sources)]
        if chunks > 1:
            total = edge_sum(3, length, counts, m_list, far[:-1], *common, total, ())
        total, fresh = tie(total, fresh)
        outs_other += fresh
        agg = edge_sum(4, 2 * length, counts, m_list, far[-1:], *common, total, parts)
    xm, _, send = mix_halves(
        chunks,
        True,
        core,
        agg,
        xm,
        xt,
        outs[ROUNDS],
        outs_other[ROUNDS],
        gains[ROUNDS],
        gains_other[ROUNDS],
        dec_weights[0],
    )
    (agg,) = edge_sum(1, 0, counts, d_list, send, grid_take, d_off, d_w, None, [rows])
    xm, agg = tie(xm, agg)
    other = swap(agg)
    mesh_out = joined_rows(xm)
    mesh_out, other = tie(mesh_out, other)
    update = update_of(core, agg, other, outs[3], outs_other[3], dec_gain[None, :])
    return place_rows(grid_order, exchange(update), grid_latent), mesh_out


def solution(mesh):
    in_specs = (
        P("nodes", "feat"),
        P("nodes", "feat"),
        P("nodes", None),
        P("nodes"),
        P("nodes"),
        P("nodes", None, None),
        P("nodes", None),
        P("nodes"),
        P("nodes"),
        P("nodes"),
        P("nodes", None, None),
        P("nodes", None),
        P("nodes"),
        P("nodes"),
        P("nodes"),
        P("nodes", None, None),
        P("nodes", None),
        P("nodes"),
        P(),
        P(None, None, "feat"),
        P(None, None, None, "feat"),
        P(None, None, "feat"),
        P("feat"),
        P("feat"),
        P(None, "feat"),
        P(None, "feat"),
        P("feat"),
        P("feat"),
    )
    out_specs = (P("nodes", "feat"), P("nodes", "feat"))
    return jax.shard_map(
        local, mesh=mesh, in_specs=in_specs, out_specs=out_specs, check_vma=False
    )
```
